32 devices in a mesh: gx: 8 (over z, y), gy: 4 (over x, core).
Axes of the slice: x: 2, y: 2, z: 4, core: 2. Of those that a mesh axis runs over, the one named last changes fastest.
Arguments:
- emb_table: float32 [65536, 128], P(('gx', 'gy')), may hold values from -0.6 to 0.6
- row_state: float32 [65536], P(('gx', 'gy')), may hold values from 1e-05 to 0.001
- pair_mask: int32 [8], P('gx'), may hold values from 0 to 3
- look_rows: int32 [196608], P(('gx', 'gy')), may hold values from 0 to 2047
- bag_sizes: int32 [32, 2048], P(('gx', 'gy')), may hold values from 1 to 12, 6144 in all within a row
- bag_owner: int32 [65536, 1], P(('gx', 'gy')), may hold values from 0 to 31, as said below
- bag_slot: int32 [65536], P(('gx', 'gy')), may hold values from 0 to 2047, as said below
- dense_vectors: float32 [4096, 128], P(('gx', 'gy')), may hold values from -3 to 3
- labels: float32 [4096], P(('gx', 'gy')), may hold values from 0 to 1
- top_weight: float32 [264, 1024], replicated, may hold values from -0.375 to 0.375
- out_weight: float32 [1024], replicated, may hold values from -0.1875 to 0.1875
Outputs:
- moved_table: float32 [65536, 128], P(('gx', 'gy'))
- moved_state: float32 [65536], P(('gx', 'gy'))
- top_grad: float32 [264, 1024], replicated
- out_grad: float32 [1024], replicated
The draws below stay inside these ranges and needn't reach their ends.
Inputs may be any that keep to these rules, and one draw needn't show every extreme that they name: Device (g, y) trades with device (g, y xor pair_mask[g]); 0 keeps the block. `look_rows`: a row of the block that the device holds after the trade. `bag_sizes`: each device's sizes sum to 6144. `bag_owner`: among one device's 2048 bags every owner is named either never or exactly 128 times; each owner is named so by exactly half of the devices. `bag_slot`: sample times 16 plus feature; the bags that reach one owner name every one of its slots exactly once.
All inputs are finite; a program needn't handle non-finite values.
Results may differ from the reference program's by a relative error of at most 0.0003.
Values sent between devices are 32-bit elements; how exact they have to be, the bound alone decides.
No kernel may reach another device: no remote copies, remote signals or barrier semaphores. Data moves between devices by JAX's collectives and lax.ppermute only.
A program may use at most 64 MiB of HBM per device.

```python
import math
import jax
import jax.numpy as jnp
import numpy as np
from jax import lax

E = 128
F = 16
H1 = 1024
ROWS_DEV = 2048
B_DEV = 128
BAG_MOST = 12
BAGS_DEV = 2048
LOOK_DEV = 6144
CAP = 128
INTER = 264
ROWS = 65536
SAMPLES = 4096
N_GX = 8
N_GY = 4
DEVICES = 32


def plan_routes(key):
    folded = jax.random.fold_in(key, 7001)
    first_key, second_key, third_key = jax.random.split(folded, 3)
    offsets = jax.random.permutation(first_key, DEVICES).astype(jnp.int32)
    ordering = jax.vmap(lambda k: jax.random.permutation(k, BAGS_DEV))(jax.random.split(second_key, DEVICES)).astype(jnp.int32)
    owners = (offsets[:, None] + ordering // CAP) % DEVICES
    spread = jax.vmap(lambda k: jax.random.permutation(k, BAGS_DEV))(jax.random.split(third_key, DEVICES)).astype(jnp.int32)
    slots = spread[owners, ordering] % (B_DEV * F)
    return (owners.astype(jnp.int32), slots.astype(jnp.int32))


def draw_bag_owner(key, part):
    owners, slots = plan_routes(key)
    return owners.reshape(DEVICES * BAGS_DEV, 1)


def draw_bag_slot(key, part):
    owners, slots = plan_routes(key)
    return slots.reshape(DEVICES * BAGS_DEV)


def with_ends(values, key, smallest, top_value):
    longest = values.shape.index(max(values.shape))
    spots = []
    for shift in (0, 1):
        where = [jax.random.randint(jax.random.fold_in(key, axis), (), 0, length) for axis, length in enumerate(values.shape)]
        where[longest] = (where[longest] + shift) % values.shape[longest]
        spots.append(tuple(where))
    return values.at[spots[0]].set(smallest).at[spots[1]].set(top_value)


def steps_of(stream_key, extent, shards, least, high):
    gain, own = 1.0, jax.random.fold_in(stream_key, 6)
    for dim, blocks in shards:
        steps = jnp.exp(jax.random.uniform(jax.random.fold_in(own, dim), (blocks,), jnp.float32, least / len(shards), high / len(shards)))
        gain = gain * jnp.repeat(steps, extent[dim] // blocks).reshape([-1 if axis == dim else 1 for axis in range(len(extent))])
    return gain


def rank_bounds(amount, slope):
    loads = [(1 << 20) // math.isqrt(grade ** slope) + 1 for grade in range(1, amount + 1)]
    deviation = 1 + sum(loads) // (1 << 30)
    return np.cumsum(np.array([max(1, weight // deviation) for weight in loads]))


def ranked_ids(stream_key, dims, number_of, lean):
    listing = rank_bounds(number_of, lean)
    lot = jax.random.randint(jax.random.fold_in(stream_key, 1), dims, 0, int(listing[number_of - 1]))
    rank = jnp.searchsorted(jnp.asarray(listing, jnp.int32), lot, side="right")
    return jax.random.permutation(jax.random.fold_in(stream_key, 2), number_of)[rank].astype(jnp.int32)


def length_profile(number_of, total, bound, slope):
    weights = [(1 << 20) // math.isqrt(rank ** slope) + 1 for rank in range(2, number_of + 1)]
    surplus, given = total - bound - (number_of - 1), [1] * (number_of - 1)
    while surplus > 0:
        candidates = [i for i in range(number_of - 1) if given[i] < bound]
        pool, budget = sum([weights[i] for i in candidates]), surplus
        for i in candidates:
            extra = min(bound - given[i], max(1, budget * weights[i] // pool), surplus)
            given[i] = given[i] + extra
            surplus = surplus - extra
    return np.array([bound] + given)


def ragged(rng, count, total, limit, slope):
    if count == 2:
        one = jax.random.randint(rng, (), max(1, total - limit), min(limit, total - 1) + 1)
        return jnp.stack([one, total - one])
    lengths = jnp.asarray(length_profile(count, total, limit, slope), jnp.int32)
    couples = (count - 1) // 2
    donor, taker = lengths[1:1 + 2 * couples:2], lengths[2:2 + 2 * couples:2]
    slack = jnp.minimum(donor - 1, limit - taker)
    shifted = jax.random.randint(jax.random.fold_in(rng, 1), (couples,), 0, 1 << 20) % (slack + 1)
    lengths = lengths.at[1:1 + 2 * couples:2].set(donor - shifted).at[2:2 + 2 * couples:2].set(taker + shifted)
    return lengths[jax.random.permutation(jax.random.fold_in(rng, 2), count)]


def centred(rng, dims, scale, limit, cuts=(), kind=jnp.bfloat16):
    values = scale * jax.random.normal(rng, dims, jnp.float32)
    if cuts:
        values = values * steps_of(rng, dims, cuts, -0.22, 0.18)
    return jnp.clip(values, -limit, limit).astype(kind)


def setup_inputs(seed: int = 0) -> dict:
    key_of = jax.random.split(jax.random.key(seed), 12)
    emb_table = centred(key_of[0], (ROWS, E), 0.1, 0.6, ((0, 32),), jnp.float32)
    row_state = jnp.clip(jnp.exp(math.log(0.001) - 4.6051703 * jax.random.uniform(key_of[1], (ROWS,), jnp.float32) ** steps_of(key_of[1], (ROWS,), ((0, 32),), -0.2, 0.2)), 9.999999747378752e-06, 0.001)
    pair_mask = with_ends(jax.random.randint(key_of[2], (N_GX,), 0, N_GY), jax.random.fold_in(key_of[2], 1), 0, N_GY - 1).astype(jnp.int32)
    look_rows = with_ends(ranked_ids(key_of[3], (DEVICES * LOOK_DEV,), ROWS_DEV, 2), jax.random.fold_in(key_of[3], 3), 0, ROWS_DEV - 1).astype(jnp.int32)
    bag_sizes = jax.vmap(lambda own: ragged(own, BAGS_DEV, LOOK_DEV, BAG_MOST, 1))(jax.random.split(key_of[4], DEVICES)).reshape((DEVICES, BAGS_DEV)).astype(jnp.int32)
    bag_owner = draw_bag_owner(jax.random.fold_in(key_of[11], 71), 0)
    bag_slot = draw_bag_slot(jax.random.fold_in(key_of[11], 71), 0)
    dense_vectors = centred(key_of[7], (SAMPLES, E), 0.5, 3.0, ((0, 32),), jnp.float32)
    labels = jnp.clip(1.0 * jax.random.uniform(key_of[8], (SAMPLES,), jnp.float32) ** steps_of(key_of[8], (SAMPLES,), ((0, 32),), -0.2, 0.2), 0.0, 1.0)
    top_weight = centred(key_of[9], (INTER, H1), INTER ** -0.5, 0.375, (), jnp.float32)
    out_weight = centred(key_of[10], (H1,), H1 ** -0.5, 0.1875, (), jnp.float32)
    return dict(emb_table=emb_table, row_state=row_state, pair_mask=pair_mask, look_rows=look_rows, bag_sizes=bag_sizes, bag_owner=bag_owner, bag_slot=bag_slot, dense_vectors=dense_vectors, labels=labels, top_weight=top_weight, out_weight=out_weight)


learn_rate = 0.05
epsilon = 1e-08

def pair_terms(vectors):
    gram_all = jnp.einsum('bie,bje->bij', vectors, vectors, precision=lax.Precision.HIGHEST)
    upper_row, upper_col = np.triu_indices(F + 1, 1)
    return gram_all[:, upper_row, upper_col]

def sample_loss(pooled, dense_vectors, labels, top_weight, out_weight):
    sample_count = dense_vectors.shape[0]
    vectors = jnp.concatenate([dense_vectors[:, None, :], pooled.reshape(sample_count, F, E)], axis=1)
    interact = jnp.concatenate([dense_vectors, pair_terms(vectors)], axis=1)
    hidden = jax.nn.silu(jnp.dot(interact, top_weight, precision=lax.Precision.HIGHEST))
    logits = jnp.dot(hidden, out_weight, precision=lax.Precision.HIGHEST)
    return jnp.sum(jax.nn.softplus(logits) - labels * logits)

def bag_index(sizes_row, lookup_count):
    ending = jnp.cumsum(sizes_row)
    positions = jnp.arange(lookup_count, dtype=jnp.int32)
    return jnp.searchsorted(ending, positions, side='right').astype(jnp.int32)

def reference(emb_table, row_state, pair_mask, look_rows, bag_sizes, bag_owner, bag_slot, dense_vectors, labels, top_weight, out_weight):
    blocks = emb_table.reshape(N_GX, N_GY, ROWS_DEV, E)
    states = row_state.reshape(N_GX, N_GY, ROWS_DEV)
    column = jnp.arange(N_GY, dtype=jnp.int32)
    partner = jnp.bitwise_xor(column[None, :], pair_mask[:, None])
    groups = jnp.arange(N_GX, dtype=jnp.int32)[:, None]
    held_table = blocks[groups, partner].reshape(DEVICES, ROWS_DEV, E)
    held_state = states[groups, partner].reshape(DEVICES, ROWS_DEV)
    lookups = look_rows.reshape(DEVICES, LOOK_DEV)

    def pool_device(inputs):
        table_block, lookup_ids, sizes_row = inputs
        return jax.ops.segment_sum(table_block[lookup_ids], bag_index(sizes_row, LOOK_DEV), num_segments=BAGS_DEV)
    partial_value = lax.map(pool_device, (held_table, lookups, bag_sizes)).reshape(DEVICES * BAGS_DEV, E)
    target = bag_owner[:, 0] * (B_DEV * F) + bag_slot
    pooled = jax.ops.segment_sum(partial_value, target, num_segments=SAMPLES * F)
    d_pooled, top_grad, out_grad = jax.grad(sample_loss, argnums=(0, 3, 4))(pooled, dense_vectors, labels, top_weight, out_weight)
    d_partial = d_pooled[target].reshape(DEVICES, BAGS_DEV, E)

    def rows_device(inputs):
        bag_grads, lookup_ids, sizes_row = inputs
        return jax.ops.segment_sum(bag_grads[bag_index(sizes_row, LOOK_DEV)], lookup_ids, num_segments=ROWS_DEV)
    row_grad = lax.map(rows_device, (d_partial, lookups, bag_sizes))
    moved_state = held_state + lax.optimization_barrier(jnp.mean(row_grad * row_grad, axis=2))
    moved_table = held_table - learn_rate * row_grad / (jnp.sqrt(moved_state)[:, :, None] + epsilon)
    return (moved_table.reshape(ROWS, E), moved_state.reshape(ROWS), top_grad, out_grad)
```

```python
import functools

import jax
import jax.numpy as jnp
from jax import lax
from jax.experimental import pallas as pl
from jax.experimental.pallas import tpu as pltpu
from jax.sharding import PartitionSpec as P

AXES = ("gx", "gy")
LANES = 128
TILE = 256
WINDOW = TILE + 8
learn_rate = 0.05
epsilon = 1e-08
HIGHEST = lax.Precision.HIGHEST
F32 = jnp.float32
BF16 = jnp.bfloat16
VMEM = pl.BlockSpec(memory_space=pltpu.VMEM)
SMEM = pl.BlockSpec(memory_space=pltpu.SMEM)


def iota(shape, axis):
    return lax.broadcasted_iota(jnp.int32, shape, axis)


def ones_where(mask):
    return jnp.where(mask, 1.0, 0.0).astype(BF16)


def dot(a, b, **kw):
    return jnp.dot(a, b, preferred_element_type=F32, **kw)


def dot_t(a, b, **kw):
    return lax.dot_general(a, b, (((1,), (1,)), ((), ())), preferred_element_type=F32, **kw)


def split(x):
    high = x.astype(BF16)
    low = (x - high.astype(F32)).astype(BF16)
    return jnp.concatenate([high, low], axis=1)


def fold(x):
    half = x.shape[1] // 2
    return x[:, :half] + x[:, half:]


def prep_kernel(devices, capacity, features, look_ref, sizes_ref, owner_ref, slot_ref, meta_ref, slots_ref):
    look_tiles = look_ref.shape[0]
    rows = sizes_ref.shape[0]
    samples = rows * LANES // features
    sizes = sizes_ref[...].astype(F32)
    owner = owner_ref[...]
    slot = slot_ref[...]
    lane_row, lane_col = iota((LANES, LANES), 0), iota((LANES, LANES), 1)
    upto = ones_where(lane_row <= lane_col)
    before = ones_where(lane_row < lane_col)
    every = jnp.ones((LANES, LANES), BF16)
    earlier = jnp.where(iota((rows, rows), 1) < iota((rows, rows), 0), 1.0, 0.0)
    sizes_b = sizes.astype(BF16)
    ends = dot(sizes_b, upto) + dot(earlier, dot(sizes_b, every), precision=HIGHEST)
    ends_i = ends.astype(jnp.int32)
    meta_ref[:look_tiles] = look_ref[...]
    meta_ref[look_tiles : look_tiles + rows] = (ends - sizes).astype(jnp.int32)
    meta_ref[look_tiles + rows : look_tiles + 2 * rows] = ends_i
    masks = [jnp.where(owner == d, 1.0, 0.0) for d in range(devices)]
    stack = jnp.concatenate(masks, axis=0).astype(BF16)
    ahead = dot(stack, before)
    total = dot(stack, every).astype(BF16)
    block = LANES // rows
    chain = ones_where((lane_row // rows == lane_col // rows) & (lane_col < lane_row))
    rank = jnp.zeros((rows, LANES), F32)
    for first in range(0, devices, block):
        part = slice(first * rows, (first + block) * rows)
        place = ahead[part] + dot(chain, total[part])
        for d in range(block):
            rank += masks[first + d] * place[d * rows : (d + 1) * rows]
    rank_i = rank.astype(jnp.int32)
    meta_ref[look_tiles + 2 * rows : look_tiles + 3 * rows] = owner * capacity + rank_i
    lane = iota((1, LANES), 1)
    starting = jnp.zeros((1, LANES), jnp.int32)
    for t in range(look_tiles * LANES // TILE):
        done = jnp.where(ends_i <= t * TILE, 1, 0)
        done = jnp.sum(jnp.sum(done, axis=0, keepdims=True), axis=1, keepdims=True)
        starting = jnp.where(lane == t, (done // 8) * 8, starting)
    meta_ref[look_tiles + 3 * rows :] = jnp.broadcast_to(starting, (8, LANES))
    where_to = (slot % features) * samples + slot // features
    high, low = (where_to // 64).astype(F32), (where_to % 64).astype(F32)
    found = jnp.zeros((3 * devices, LANES), F32)
    device_row = iota((devices, LANES), 0)
    for i in range(rows):
        mine = jnp.where(owner[i : i + 1] == device_row, 1.0, 0.0)
        left = jnp.concatenate([mine * high[i : i + 1], mine * low[i : i + 1], mine], axis=0).astype(BF16)
        found += dot_t(left, ones_where(rank_i[i : i + 1] == lane_row))
    value = found[:devices] * 64 + found[devices : 2 * devices]
    slots_ref[...] = jnp.where(found[2 * devices :] > 0.5, value, -1.0).astype(jnp.int32)


def column(row):
    return jnp.broadcast_to(row, (LANES, LANES)).T


def pool_kernel(look_tiles, rows, meta_s, meta_v, table, out, gathered, pooled, first_k, last_k):
    bags = rows * LANES
    meta = meta_v[look_tiles : look_tiles + 2 * rows].astype(F32)
    for i in range(rows):
        at = slice(i * LANES, (i + 1) * LANES)
        first_k[at] = column(meta[i : i + 1])
        last_k[at] = column(meta[rows + i : rows + i + 1])
    first_k[bags:] = jnp.full((WINDOW, LANES), 1e9, F32)
    last_k[bags:] = jnp.full((WINDOW, LANES), -1.0, F32)
    pooled[...] = jnp.zeros_like(pooled)

    @pl.loop(0, look_tiles)
    def _(r):
        base = pl.multiple_of(r * LANES, LANES)
        for c in range(LANES):
            gathered[pl.ds(base + c, 1)] = table[pl.ds(meta_s[r, c], 1)]

    lane = iota((WINDOW, LANES), 1).astype(F32)
    for t in range(look_tiles * LANES // TILE):
        window = pl.ds(pl.multiple_of(meta_s[look_tiles + 3 * rows, t], 8), WINDOW)
        first, last = first_k[window], last_k[window]
        parts = []
        for h in range(TILE // LANES):
            k = lane + (t * TILE + h * LANES)
            parts.append(ones_where((k >= first) & (k < last)))
        chosen = jnp.concatenate(parts, axis=1)
        pooled[window] += fold(dot(chosen, split(gathered[t * TILE : (t + 1) * TILE])))

    @pl.loop(0, rows)
    def _(r):
        base = pl.multiple_of(r * LANES, LANES)
        for c in range(LANES):
            out[pl.ds(meta_s[look_tiles + 2 * rows + r, c], 1)] = pooled[pl.ds(base + c, 1)]


def count_kernel(look_tiles, rows, meta_s, meta_v, out, total):
    i = pl.program_id(0)
    per = TILE // LANES
    start_row = look_tiles + i * per
    lowest = meta_s[start_row, 0]
    highest = meta_s[start_row + rows + per - 1, LANES - 1]
    starts = jnp.concatenate([meta_v[pl.ds(start_row + h, 1)] for h in range(per)], axis=1)
    ends = jnp.concatenate([meta_v[pl.ds(start_row + rows + h, 1)] for h in range(per)], axis=1)
    total[...] = jnp.zeros_like(total)

    @pl.loop(lowest // TILE, (highest + TILE - 1) // TILE)
    def _(c):
        look = jnp.concatenate([meta_v[pl.ds(c * per + h, 1)] for h in range(per)], axis=1)
        k = iota((TILE, TILE), 0) + c * TILE
        member = ones_where((k >= starts) & (k < ends))
        picked = ones_where(iota((total.shape[0], TILE), 0) == look)
        total[...] += dot(picked, member)

    out[...] = total[...].astype(BF16)


def dense_kernel(features, capacity, slots, source, got, dense, labels, weight, out_weight, back, interact_ref, d_pre_ref, out_grad, vectors, d_vectors, d_pairs):
    devices = slots.shape[0]
    samples = dense.shape[0]
    row_of = [(i, j) for i in range(features + 1) for j in range(i + 1, features + 1)]

    @pl.loop(0, devices)
    def _(s):
        @pl.when(slots[s, 0] >= 0)
        def _():
            base = source[s] * capacity
            for j in range(capacity):
                vectors[pl.ds(slots[s, j], 1)] = got[pl.ds(base + j, 1)]

    interact_ref[:, :LANES] = dense[...]
    lane = iota((8, LANES), 1)

    @pl.loop(0, samples // 8)
    def _(t):
        at = pl.multiple_of(t * 8, 8)
        each = [dense[pl.ds(at, 8)]] + [vectors[pl.ds(f * samples + at, 8)] for f in range(features)]
        tiles = [jnp.zeros((8, LANES), F32) for _ in range(2)]
        for p, (i, j) in enumerate(row_of):
            inner = jnp.sum(each[i] * each[j], axis=1, keepdims=True)
            tiles[p // LANES] = jnp.where(lane == p % LANES, inner, tiles[p // LANES])
        interact_ref[pl.ds(at, 8), LANES:] = jnp.concatenate(tiles, axis=1)

    pre = dot(interact_ref[...], weight[...], precision=HIGHEST)
    gate = 1.0 / (1.0 + jnp.exp(-pre))
    hidden = pre * gate
    logits = jnp.sum(hidden * out_weight[...], axis=1, keepdims=True)
    label = column(labels[...])[:, :1]
    d_logits = 1.0 / (1.0 + jnp.exp(-logits)) - label
    out_grad[...] = jnp.sum(hidden * d_logits, axis=0, keepdims=True)
    d_pre = d_logits * out_weight[...] * (gate * (1.0 + pre * (1.0 - gate)))
    d_pre_ref[...] = d_pre
    d_pairs[...] = dot_t(d_pre, weight[LANES:], precision=HIGHEST)

    @pl.loop(0, samples // 8)
    def _(t):
        at = pl.multiple_of(t * 8, 8)
        each = [dense[pl.ds(at, 8)]] + [vectors[pl.ds(f * samples + at, 8)] for f in range(features)]
        slopes = d_pairs[pl.ds(at, 8)]
        sums = [None] * (features + 1)
        for p, (i, j) in enumerate(row_of):
            slope = jnp.broadcast_to(slopes[:, p : p + 1], (8, LANES))
            if i > 0:
                sums[i] = slope * each[j] if sums[i] is None else sums[i] + slope * each[j]
            sums[j] = slope * each[i] if sums[j] is None else sums[j] + slope * each[i]
        for f in range(features):
            d_vectors[pl.ds(f * samples + at, 8)] = sums[f + 1]

    @pl.loop(0, devices)
    def _(s):
        @pl.when(slots[s, 0] >= 0)
        def _():
            base = s * capacity
            for j in range(capacity):
                back[pl.ds(base + j, 1)] = d_vectors[pl.ds(slots[s, j], 1)]


def update_kernel(pos_s, came, counts, table, state, new_table, new_state, grads, halves):
    bag_rows = pos_s.shape[0]

    @pl.when(pl.program_id(0) == 0)
    def _():
        @pl.loop(0, bag_rows)
        def _(r):
            base = pl.multiple_of(r * LANES, LANES)
            for c in range(LANES):
                grads[pl.ds(base + c, 1)] = came[pl.ds(pos_s[r, c], 1)]

        halves[...] = split(grads[...])

    row_grad = fold(dot(counts[...], halves[...]))
    width = row_grad.shape[1]
    for j in range(state.shape[0]):
        at = slice(j * LANES, (j + 1) * LANES)
        grad = row_grad[at]
        moved = column(state[j : j + 1]) + jnp.sum(grad * grad, axis=1, keepdims=True) / width
        new_table[at] = table[at] - learn_rate * grad / (jnp.sqrt(moved) + epsilon)
        new_state[j : j + 1] = moved.T[:1]


def trade(values, pair_value):
    result = values
    for bit in range(lax.axis_size("gy").bit_length() - 1):
        route = [(y, y ^ 1 << bit) for y in range(lax.axis_size("gy"))]
        partner = jax.tree.map(lambda x: lax.ppermute(x, "gy", route), result)
        flipped = jnp.bitwise_and(jnp.right_shift(pair_value, bit), 1) == 1
        result = jax.tree.map(functools.partial(jnp.where, flipped), partner, result)
    return result


def exchange(x):
    return lax.all_to_all(x, AXES, split_axis=0, concat_axis=0, tiled=True)


def sum_everywhere(x):
    devices = lax.axis_size("gx") * lax.axis_size("gy")
    me = lax.axis_index(AXES)
    groups, low, bits = [], 0, devices.bit_length() - 1
    while low < bits:
        width = 1 if low == 0 else min(2, bits - low)
        groups.append((low, width))
        low += width

    def swap(value, offset):
        return lax.ppermute(value, AXES, [(d, d ^ offset) for d in range(devices)])

    def stage(value, at):
        if at == len(groups):
            return value
        low, width = groups[at]
        count, axis = 1 << width, 1 - at % 2
        size = value.shape[axis] // count
        mine = jnp.bitwise_and(jnp.right_shift(me, low), count - 1)

        def piece(index):
            return lax.dynamic_slice_in_dim(value, index * size, size, axis)

        total = piece(mine)
        for k in range(1, count):
            total = total + swap(piece(jnp.bitwise_xor(mine, k)), k << low)
        total = stage(total, at + 1)
        result = lax.dynamic_update_slice_in_dim(jnp.zeros_like(value), total, mine * size, axis)
        for k in range(1, count):
            result = lax.dynamic_update_slice_in_dim(
                result, swap(total, k << low), jnp.bitwise_xor(mine, k) * size, axis
            )
        return result

    return stage(x, 0)


def on_device(
    emb_table, row_state, pair_mask, look_rows, bag_sizes, bag_owner, bag_slot, dense_vectors, labels, top_weight, out_weight
):
    groups_y = lax.axis_size("gy")
    devices = lax.axis_size("gx") * groups_y
    table_rows, width = emb_table.shape
    bags = bag_slot.shape[0]
    capacity = 2 * bags // devices
    samples = dense_vectors.shape[0]
    features = bags // samples
    look_tiles, rows = look_rows.shape[0] // LANES, bags // LANES
    inter, hidden = top_weight.shape
    padded = width + 2 * LANES
    pair_value = pair_mask[0]
    shape = jax.ShapeDtypeStruct

    meta, slots = pl.pallas_call(
        functools.partial(prep_kernel, devices, capacity, features),
        out_shape=(shape((look_tiles + 3 * rows + 8, LANES), jnp.int32), shape((devices, LANES), jnp.int32)),
        in_specs=[VMEM] * 4,
        out_specs=(VMEM, VMEM),
        name="prep",
    )(
        look_rows.reshape(look_tiles, LANES),
        bag_sizes.reshape(rows, LANES),
        bag_owner.reshape(rows, LANES),
        bag_slot.reshape(rows, LANES),
    )
    traded_meta = trade(meta, pair_value)
    told = jnp.stack([slots[:, :capacity], jnp.full((devices, capacity), pair_value)], axis=1)
    told = exchange(told)
    got_slots = told[:, 0]
    source = jnp.bitwise_xor(jnp.arange(devices, dtype=jnp.int32), told[:, 1, 0])

    sent = pl.pallas_call(
        functools.partial(pool_kernel, look_tiles, rows),
        out_shape=shape((devices * capacity, width), F32),
        in_specs=[SMEM, VMEM, VMEM],
        out_specs=VMEM,
        scratch_shapes=[
            pltpu.VMEM((look_tiles * LANES, width), F32),
            pltpu.VMEM((bags + WINDOW, width), F32),
            pltpu.VMEM((bags + WINDOW, LANES), F32),
            pltpu.VMEM((bags + WINDOW, LANES), F32),
        ],
        name="pool",
    )(traded_meta, traded_meta, emb_table)
    got = exchange(sent.reshape(devices, capacity, width)).reshape(devices * capacity, width)

    held_table, held_state = trade((emb_table, row_state.reshape(-1, LANES)), pair_value)
    counts = pl.pallas_call(
        functools.partial(count_kernel, look_tiles, rows),
        out_shape=shape((table_rows, bags), BF16),
        grid=(bags // TILE,),
        in_specs=[SMEM, VMEM],
        out_specs=pl.BlockSpec((table_rows, TILE), lambda i: (0, i)),
        scratch_shapes=[pltpu.VMEM((table_rows, TILE), F32)],
        name="count",
    )(meta, meta)

    weight = jnp.pad(top_weight, ((0, padded - inter), (0, 0)))
    back, interact, d_pre, out_local = pl.pallas_call(
        functools.partial(dense_kernel, features, capacity),
        out_shape=(
            shape((devices * capacity, width), F32),
            shape((samples, padded), F32),
            shape((samples, hidden), F32),
            shape((1, hidden), F32),
        ),
        in_specs=[SMEM, SMEM] + [VMEM] * 5,
        out_specs=(VMEM,) * 4,
        scratch_shapes=[
            pltpu.VMEM((bags, width), F32),
            pltpu.VMEM((bags, width), F32),
            pltpu.VMEM((samples, 2 * LANES), F32),
        ],
        name="dense",
    )(got_slots, source, got, dense_vectors, labels.reshape(1, samples), weight, out_weight.reshape(1, hidden))
    came = exchange(back.reshape(devices, capacity, width)).reshape(devices * capacity, width)

    top_local = lax.dot_general(
        interact[:, :inter], d_pre, (((0,), (0,)), ((), ())), precision=HIGHEST, preferred_element_type=F32
    )
    local = jnp.concatenate([top_local, out_local, jnp.zeros((288 - inter - 1, hidden), F32)], axis=0)
    summed = sum_everywhere(local)

    halves = 2
    new_table, new_state = pl.pallas_call(
        update_kernel,
        out_shape=(shape((table_rows, width), F32), shape((table_rows // LANES, LANES), F32)),
        grid=(halves,),
        in_specs=[
            SMEM,
            VMEM,
            pl.BlockSpec((table_rows // halves, bags), lambda i: (i, 0)),
            pl.BlockSpec((table_rows // halves, width), lambda i: (i, 0)),
            pl.BlockSpec((table_rows // LANES // halves, LANES), lambda i: (i, 0)),
        ],
        out_specs=(
            pl.BlockSpec((table_rows // halves, width), lambda i: (i, 0)),
            pl.BlockSpec((table_rows // LANES // halves, LANES), lambda i: (i, 0)),
        ),
        scratch_shapes=[pltpu.VMEM((bags, width), F32), pltpu.VMEM((bags, 2 * width), BF16)],
        name="update",
    )(meta[look_tiles + 2 * rows : look_tiles + 3 * rows], came, counts, held_table, held_state)
    return new_table, new_state.reshape(-1), summed[:inter], summed[inter]


def solution(mesh):
    both = P(AXES)
    in_specs = (P(AXES, None), both, P("gx"), both, P(AXES, None), P(AXES, None), both, P(AXES, None), both, P(), P())
    out_specs = (P(AXES, None), both, P(), P())
    return jax.shard_map(on_device, mesh=mesh, in_specs=in_specs, out_specs=out_specs, check_vma=False)
```

```python
import functools

import jax
import jax.numpy as jnp
from jax import lax
from jax.experimental import pallas as pl
from jax.experimental.pallas import tpu as pltpu
from jax.sharding import PartitionSpec as P


AXES = ("gx", "gy")
LANES = 128
TILE = 256
WINDOW = TILE + 8
learn_rate = 0.05
epsilon = 1e-08
HIGHEST = lax.Precision.HIGHEST
F32 = jnp.float32
BF16 = jnp.bfloat16
VMEM = pl.BlockSpec(memory_space=pltpu.VMEM)
SMEM = pl.BlockSpec(memory_space=pltpu.SMEM)
ANY = pl.BlockSpec(memory_space=pl.ANY)


def iota(shape, axis):
    return lax.broadcasted_iota(jnp.int32, shape, axis)


def ones_where(mask):
    return jnp.where(mask, 1.0, 0.0).astype(BF16)


def dot(a, b, **kw):
    return jnp.dot(a, b, preferred_element_type=F32, **kw)


def dot_t(a, b, **kw):
    return lax.dot_general(a, b, (((1,), (1,)), ((), ())), preferred_element_type=F32, **kw)


def split(x):
    high = x.astype(BF16)
    low = (x - high.astype(F32)).astype(BF16)
    return jnp.concatenate([high, low], axis=1)


def fold(x):
    half = x.shape[1] // 2
    return x[:, :half] + x[:, half:]


def prep_kernel(devices, capacity, features, look_ref, sizes_ref, owner_ref, slot_ref, dense_ref, labels_ref, meta_ref, slots_ref, bags_ref, told_ref):
    look_tiles = look_ref.shape[0]
    rows = sizes_ref.shape[0]
    samples = rows * LANES // features
    sizes = sizes_ref[...].astype(F32)
    owner = owner_ref[...]
    slot = slot_ref[...]
    lane_row, lane_col = iota((LANES, LANES), 0), iota((LANES, LANES), 1)
    upto = ones_where(lane_row <= lane_col)
    before = ones_where(lane_row < lane_col)
    every = jnp.ones((LANES, LANES), BF16)
    earlier = jnp.where(iota((rows, rows), 1) < iota((rows, rows), 0), 1.0, 0.0)
    sizes_b = sizes.astype(BF16)
    ends = dot(sizes_b, upto) + dot(earlier, dot(sizes_b, every), precision=HIGHEST)
    ends_i = ends.astype(jnp.int32)
    meta_ref[:look_tiles] = look_ref[...]
    meta_ref[look_tiles : look_tiles + rows] = (ends - sizes).astype(jnp.int32)
    meta_ref[look_tiles + rows : look_tiles + 2 * rows] = ends_i
    masks = [jnp.where(owner == d, 1.0, 0.0) for d in range(devices)]
    stack = jnp.concatenate(masks, axis=0).astype(BF16)
    ahead = dot(stack, before)
    total = dot(stack, every).astype(BF16)
    block = LANES // rows
    chain = ones_where((lane_row // rows == lane_col // rows) & (lane_col < lane_row))
    rank = jnp.zeros((rows, LANES), F32)
    for first in range(0, devices, block):
        part = slice(first * rows, (first + block) * rows)
        place = ahead[part] + dot(chain, total[part])
        for d in range(block):
            rank += masks[first + d] * place[d * rows : (d + 1) * rows]
    rank_i = rank.astype(jnp.int32)
    meta_ref[look_tiles + 2 * rows : look_tiles + 3 * rows] = owner * capacity + rank_i
    lane = iota((1, LANES), 1)
    starting = jnp.zeros((1, LANES), jnp.int32)
    for t in range(look_tiles * LANES // TILE):
        done = jnp.where(ends_i <= t * TILE, 1, 0)
        done = jnp.sum(jnp.sum(done, axis=0, keepdims=True), axis=1, keepdims=True)
        starting = jnp.where(lane == t, (done // 8) * 8, starting)
    meta_ref[look_tiles + 3 * rows :] = jnp.broadcast_to(starting, (8, LANES))
    where_to = (slot % features) * samples + slot // features
    high, low = (where_to // 64).astype(F32), (where_to % 64).astype(F32)
    found = jnp.zeros((5 * devices, LANES), F32)
    device_row = iota((devices, LANES), 0)
    across = iota((1, LANES), 1).astype(F32)
    for i in range(rows):
        mine = jnp.where(owner[i : i + 1] == device_row, 1.0, 0.0)
        left = jnp.concatenate(
            [mine * high[i : i + 1], mine * low[i : i + 1], mine, mine * float(i), mine * across], axis=0
        ).astype(BF16)
        found += dot_t(left, ones_where(rank_i[i : i + 1] == lane_row))
    found = [found[n * devices : (n + 1) * devices] for n in range(5)]
    slots_ref[...] = jnp.where(found[2] > 0.5, found[0] * 64 + found[1], -1.0).astype(jnp.int32)
    bags_ref[...] = jnp.where(found[2] > 0.5, found[3] * LANES + found[4], -1.0).astype(jnp.int32)
    told_ref[:samples] = dense_ref[...]
    told_ref[samples:] = jnp.broadcast_to(labels_ref[...], (8, LANES))


def column(row):
    return jnp.broadcast_to(row, (LANES, LANES)).T


def pool_kernel(look_tiles, rows, meta_s, meta_v, table, out, even, odd, pooled, first_k, last_k):
    bags = rows * LANES
    steps = look_tiles * LANES // TILE
    meta = meta_v[look_tiles : look_tiles + 2 * rows].astype(F32)
    for i in range(rows):
        at = slice(i * LANES, (i + 1) * LANES)
        first_k[at] = column(meta[i : i + 1])
        last_k[at] = column(meta[rows + i : rows + i + 1])
    first_k[bags:] = jnp.full((WINDOW, LANES), 1e9, F32)
    last_k[bags:] = jnp.full((WINDOW, LANES), -1.0, F32)
    pooled[...] = jnp.zeros_like(pooled)
    lane = iota((WINDOW, LANES), 1)

    def add_tile(t, source):
        window = pl.ds(pl.multiple_of(meta_s[look_tiles + 3 * rows, t], 8), WINDOW)
        first, last = first_k[window], last_k[window]
        parts = []
        for h in range(TILE // LANES):
            k = (lane + (t * TILE + h * LANES)).astype(F32)
            parts.append(ones_where((k >= first) & (k < last)))
        chosen = jnp.concatenate(parts, axis=1)
        pooled[window] += fold(dot(chosen, split(source[...])))

    def pick_tile(t, target):
        for c in range(TILE):
            target[c : c + 1] = table[pl.ds(meta_s[t * (TILE // LANES) + c // LANES, c % LANES], 1)]

    buffers = (even, odd)
    pick_tile(0, even)
    for t in range(1, steps):
        pick_tile(t, buffers[t % 2])
        add_tile(t - 1, buffers[(t - 1) % 2])
    add_tile(steps - 1, buffers[(steps - 1) % 2])

    for r in range(rows):
        for c in range(LANES):
            out[pl.ds(meta_s[look_tiles + 2 * rows + r, c], 1)] = pooled[r * LANES + c : r * LANES + c + 1]


def count_kernel(look_tiles, rows, meta_s, meta_v, out, total):
    i = pl.program_id(0)
    per = TILE // LANES
    start_row = look_tiles + i * per
    lowest = meta_s[start_row, 0]
    highest = meta_s[start_row + rows + per - 1, LANES - 1]
    starts = jnp.concatenate([meta_v[pl.ds(start_row + h, 1)] for h in range(per)], axis=1)
    ends = jnp.concatenate([meta_v[pl.ds(start_row + rows + h, 1)] for h in range(per)], axis=1)
    total[...] = jnp.zeros_like(total)

    @pl.loop(lowest // TILE, (highest + TILE - 1) // TILE)
    def _(c):
        look = jnp.concatenate([meta_v[pl.ds(c * per + h, 1)] for h in range(per)], axis=1)
        k = iota((TILE, TILE), 0) + c * TILE
        member = ones_where((k >= starts) & (k < ends))
        picked = ones_where(iota((total.shape[0], TILE), 0) == look)
        total[...] += dot(picked, member)

    out[...] = total[...].astype(BF16)


def pairs_of(features):
    return [(i, j) for i in range(features + 1) for j in range(i + 1, features + 1)]


def tile_of(dense, vectors, samples, features, at):
    return [dense[pl.ds(at, 8)]] + [vectors[pl.ds(f * samples + at, 8)] for f in range(features)]


def scatter_rows(places, source, capacity, blocks, target):
    for s in range(places.shape[0]):

        @pl.when(places[s, 0] >= 0)
        def _():
            part = blocks.at[pl.ds(pl.multiple_of(source(s) * capacity, 8), capacity)]
            for j in range(capacity):
                target[pl.ds(places[s, j], 1)] = part[j : j + 1]


def gram_kernel(features, capacity, slots, source, got, dense, vectors, pairs, more):
    samples = dense.shape[0]
    scatter_rows(slots, lambda s: source[s], capacity, got, vectors)
    lane = iota((8, LANES), 1)

    @pl.loop(0, samples // 8)
    def _(t):
        at = pl.multiple_of(t * 8, 8)
        each = tile_of(dense, vectors, samples, features, at)
        tiles = [jnp.zeros((8, LANES), F32) for _ in range(2)]
        for p, (i, j) in enumerate(pairs_of(features)):
            inner = jnp.sum(each[i] * each[j], axis=1, keepdims=True)
            tiles[p // LANES] = jnp.where(lane == p % LANES, inner, tiles[p // LANES])
        pairs[pl.ds(at, 8)] = tiles[0]
        more[pl.ds(at, 8)] = tiles[1]

    pairs[samples:] = more[...].T[: pairs.shape[0] - samples]


def halves_of(x):
    high = x.astype(BF16)
    return high, (x - high.astype(F32)).astype(BF16)


def weight_kernel(weight, right, left):
    inter = weight.shape[0]
    dense_h, dense_l = halves_of(weight[:LANES])
    pairs_h, pairs_l = halves_of(weight[LANES : 2 * LANES])
    rest_h, rest_l = halves_of(weight[2 * LANES :])
    rest_h, rest_l = rest_h.astype(F32), rest_l.astype(F32)
    hidden = weight.shape[1]
    gap = jnp.zeros((LANES - 3 * (inter - 2 * LANES), hidden), F32)
    rest = jnp.concatenate([rest_h, rest_l, rest_h, gap], axis=0).astype(BF16)
    right[...] = jnp.concatenate([dense_h, pairs_h, dense_l, pairs_l, dense_h, pairs_h, rest], axis=0)
    gap = jnp.zeros((3 * LANES - inter, hidden), F32)
    tail_h = jnp.concatenate([rest_h, gap], axis=0).astype(BF16)
    tail_l = jnp.concatenate([rest_l, gap], axis=0).astype(BF16)
    for n, (head, tail) in enumerate(((pairs_h, tail_h), (pairs_l, tail_l), (pairs_h, tail_h))):
        left[:, n * hidden : (n + 1) * hidden] = jnp.concatenate([head, tail], axis=0)


def inputs_of(dense, told):
    samples = dense.shape[0]
    dense_h, dense_l = halves_of(dense)
    pairs_h, pairs_l = halves_of(told[:samples])
    tail = told[samples:]
    tail_h = tail.astype(BF16).astype(F32)
    gap = jnp.zeros((LANES - 3 * tail.shape[0], samples), F32)
    rest = jnp.concatenate([tail_h, tail_h, tail - tail_h, gap], axis=0).T.astype(BF16)
    return jnp.concatenate([dense_h, pairs_h, dense_h, pairs_h, dense_l, pairs_l, rest], axis=1)


def forward(x, labels, weight, out_weight):
    pre = dot(x, weight)
    gate = 1.0 / (1.0 + jnp.exp(-pre))
    hidden = pre * gate
    logits = jnp.sum(hidden * out_weight, axis=1, keepdims=True)
    d_logits = 1.0 / (1.0 + jnp.exp(-logits)) - labels
    d_pre = d_logits * out_weight * (gate + hidden * (1.0 - gate))
    return hidden, d_logits, d_pre


def back_kernel(features, capacity, slots, dense, vectors, pairs, labels, weight, left, out_weight, back, d_vectors, d_pairs, ready, sent):
    devices = slots.shape[0]
    samples = dense.shape[0]
    x = inputs_of(dense[...], pairs[...])
    _, _, d_pre = forward(x, column(labels[...])[:, :1], weight[...], out_weight[...])
    high, low = halves_of(d_pre)
    d_pairs[...] = dot_t(jnp.concatenate([high, high, low], axis=1), left[...])

    @pl.loop(0, samples // 8)
    def _(t):
        at = pl.multiple_of(t * 8, 8)
        each = tile_of(dense, vectors, samples, features, at)
        slopes = d_pairs[pl.ds(at, 8)]
        sums = [None] * (features + 1)
        for p, (i, j) in enumerate(pairs_of(features)):
            slope = jnp.broadcast_to(slopes[:, p : p + 1], (8, LANES))
            if i > 0:
                sums[i] = slope * each[j] if sums[i] is None else sums[i] + slope * each[j]
            sums[j] = slope * each[i] if sums[j] is None else sums[j] + slope * each[i]
        for f in range(features):
            d_vectors[pl.ds(f * samples + at, 8)] = sums[f + 1]

    def copy(s):
        part = pl.ds(pl.multiple_of(s * capacity, 8), capacity)
        return pltpu.make_async_copy(ready.at[part], back.at[part], sent.at[s])

    for s in range(devices):

        @pl.when(slots[s, 0] >= 0)
        def _(s=s):
            for j in range(s * capacity, (s + 1) * capacity):
                ready[j : j + 1] = d_vectors[pl.ds(slots[s, j - s * capacity], 1)]
            copy(s).start()

    @pl.loop(0, devices)
    def _(s):
        @pl.when(slots[s, 0] >= 0)
        def _():
            copy(s).wait()


def pack_kernel(*refs):
    size = refs[0].shape[0]
    for n, ref in enumerate(refs[:-1]):
        refs[-1][n * size : (n + 1) * size] = ref[...]


def top_kernel(parts, *refs):
    dense_refs, pairs_refs = refs[:parts], refs[parts : 2 * parts]
    weight, out_weight, grad, dense_all, pairs_all = refs[2 * parts :]
    size = dense_refs[0].shape[0]
    inter = grad.shape[0] - 8
    block = LANES + inter - 2 * LANES
    for n in range(parts):
        dense_all[n * size : (n + 1) * size] = dense_refs[n][...]
        pairs_all[n * size : (n + 1) * size] = pairs_refs[n][...]
    grad[...] = jnp.zeros_like(grad)

    @pl.loop(0, parts)
    def _(n):
        xs, labels, columns = [], [], []
        for m in range(size // block):
            at = pl.ds(pl.multiple_of(n * size + m * block, 8), block)
            rows, told = dense_all[at], pairs_all[at]
            dense = rows[:LANES]
            xs.append(inputs_of(dense, told))
            labels.append(column(rows[LANES : LANES + 1])[:, :1])
            columns.append(jnp.concatenate([dense.T, told[:LANES].T, told[LANES:], jnp.zeros((8, LANES), F32)], axis=0))
        hidden, d_logits, d_pre = forward(
            jnp.concatenate(xs, axis=0), jnp.concatenate(labels, axis=0), weight[...], out_weight[...]
        )
        x_high, x_low = halves_of(jnp.concatenate(columns, axis=1))
        d_high, d_low = halves_of(d_pre)
        grad[...] += dot(
            jnp.concatenate([x_high, x_high, x_low], axis=1), jnp.concatenate([d_high, d_low, d_high], axis=0)
        )
        grad[inter:] += jnp.broadcast_to(jnp.sum(hidden * d_logits, axis=0, keepdims=True), (8, grad.shape[1]))


def update_kernel(capacity, chunks, bags_s, came, counts, table, state, new_table, new_state, grads):
    scatter_rows(bags_s, lambda s: s, capacity, came, grads)
    parts = split(grads[...])
    width = grads.shape[1]
    size = counts.shape[0] // chunks
    for n in range(chunks):
        row_grad = fold(dot(counts[n * size : (n + 1) * size], parts))
        for j in range(size // LANES):
            tile = n * (size // LANES) + j
            at = slice(tile * LANES, (tile + 1) * LANES)
            grad = row_grad[j * LANES : (j + 1) * LANES]
            moved = column(state[tile : tile + 1]) + jnp.sum(grad * grad, axis=1, keepdims=True) / width
            new_table[at] = table[at] - learn_rate * grad / (jnp.sqrt(moved) + epsilon)
            new_state[tile : tile + 1] = moved.T[:1]


def trade(values, pair_value):
    result = values
    for bit in range(lax.axis_size("gy").bit_length() - 1):
        route = [(y, y ^ 1 << bit) for y in range(lax.axis_size("gy"))]
        partner = jax.tree.map(lambda x: lax.ppermute(x, "gy", route), result)
        flipped = jnp.bitwise_and(jnp.right_shift(pair_value, bit), 1) == 1
        result = jax.tree.map(functools.partial(jnp.where, flipped), partner, result)
    return result


def exchange(x):
    return lax.all_to_all(x, AXES, split_axis=0, concat_axis=0, tiled=True)


def in_vmem(value):
    return pltpu.with_memory_space_constraint(value, pltpu.VMEM)


def swap(value, offset):
    devices = lax.axis_size("gx") * lax.axis_size("gy")
    return lax.ppermute(value, AXES, [(d, d ^ offset) for d in range(devices)])


def gather_near(value):
    bits = (lax.axis_size("gx") * lax.axis_size("gy")).bit_length() - 1
    far = [value] + [swap(value, k << bits - 2) for k in range(1, 4)]
    value = pl.pallas_call(
        pack_kernel,
        out_shape=jax.ShapeDtypeStruct((4 * value.shape[0], value.shape[1]), value.dtype),
        in_specs=[VMEM] * 4,
        out_specs=VMEM,
    )(*far)
    return [value] + [swap(value, k << bits - 4) for k in range(1, 4)]


def sum_rest(value):
    bits = (lax.axis_size("gx") * lax.axis_size("gy")).bit_length() - 1
    for bit in range(bits - 4):
        value = value + swap(value, 1 << bit)
    return value


def on_device(
    emb_table, row_state, pair_mask, look_rows, bag_sizes, bag_owner, bag_slot, dense_vectors, labels, top_weight, out_weight
):
    groups_y = lax.axis_size("gy")
    devices = lax.axis_size("gx") * groups_y
    table_rows, width = emb_table.shape
    bags = bag_slot.shape[0]
    capacity = 2 * bags // devices
    samples = dense_vectors.shape[0]
    features = bags // samples
    look_tiles, rows = look_rows.shape[0] // LANES, bags // LANES
    inter, hidden = top_weight.shape
    pair_value = pair_mask[0]
    shape = jax.ShapeDtypeStruct

    tail = inter - 2 * LANES
    meta, slots, places, dense_told = pl.pallas_call(
        functools.partial(prep_kernel, devices, capacity, features),
        out_shape=(
            shape((look_tiles + 3 * rows + 8, LANES), jnp.int32),
            shape((devices, LANES), jnp.int32),
            shape((devices, LANES), jnp.int32),
            shape((samples + tail, width), F32),
        ),
        in_specs=[VMEM] * 6,
        out_specs=(VMEM,) * 4,
        name="prep",
    )(
        look_rows.reshape(look_tiles, LANES),
        bag_sizes.reshape(rows, LANES),
        bag_owner.reshape(rows, LANES),
        bag_slot.reshape(rows, LANES),
        dense_vectors,
        labels.reshape(1, samples),
    )
    traded_meta = trade(meta, pair_value)
    told = jnp.stack([slots[:, :capacity], jnp.full((devices, capacity), pair_value)], axis=1)
    told = exchange(told)
    got_slots = told[:, 0]
    source = jnp.bitwise_xor(jnp.arange(devices, dtype=jnp.int32), told[:, 1, 0])

    sent = pl.pallas_call(
        functools.partial(pool_kernel, look_tiles, rows),
        out_shape=shape((devices * capacity, width), F32),
        in_specs=[SMEM, VMEM, VMEM],
        out_specs=VMEM,
        scratch_shapes=[
            pltpu.VMEM((TILE, width), F32),
            pltpu.VMEM((TILE, width), F32),
            pltpu.VMEM((bags + WINDOW, width), F32),
            pltpu.VMEM((bags + WINDOW, LANES), F32),
            pltpu.VMEM((bags + WINDOW, LANES), F32),
        ],
        name="pool",
    )(traded_meta, traded_meta, emb_table)
    dense_told, sent = lax.optimization_barrier((dense_told, sent))
    got = exchange(sent.reshape(devices, capacity, width))
    got = got.reshape(devices * capacity, width)

    held_table = trade(emb_table, pair_value)
    held_state = trade(row_state.reshape(-1, LANES), pair_value)
    counts = pl.pallas_call(
        functools.partial(count_kernel, look_tiles, rows),
        out_shape=shape((table_rows, bags), BF16),
        grid=(bags // TILE,),
        in_specs=[SMEM, VMEM],
        out_specs=pl.BlockSpec((table_rows, TILE), lambda i: (0, i)),
        scratch_shapes=[pltpu.VMEM((table_rows, TILE), F32)],
        name="count",
    )(meta, meta)

    right, left = pl.pallas_call(
        weight_kernel,
        out_shape=(shape((7 * LANES, hidden), BF16), shape((2 * LANES, 3 * hidden), BF16)),
        in_specs=[VMEM],
        out_specs=(VMEM, VMEM),
        name="weights",
    )(top_weight)
    out_row = out_weight.reshape(1, hidden)
    block_scratch = [pltpu.VMEM((devices * capacity, width), F32), pltpu.SemaphoreType.DMA((devices,))]
    vectors, pairs = pl.pallas_call(
        functools.partial(gram_kernel, features, capacity),
        out_shape=(shape((bags, width), F32), shape((samples + tail, LANES), F32)),
        in_specs=[SMEM, SMEM, VMEM, VMEM],
        out_specs=(VMEM, VMEM),
        scratch_shapes=[pltpu.VMEM((samples, LANES), F32)],
        compiler_params=pltpu.CompilerParams(vmem_limit_bytes=16 << 20),
        name="gram",
    )(got_slots, source, in_vmem(got), dense_vectors)
    near_dense = gather_near(dense_told)
    near_pairs = gather_near(pairs)

    back = pl.pallas_call(
        functools.partial(back_kernel, features, capacity),
        out_shape=shape((devices * capacity, width), F32),
        in_specs=[SMEM] + [VMEM] * 7,
        out_specs=ANY,
        scratch_shapes=[pltpu.VMEM((bags, width), F32), pltpu.VMEM((samples, 2 * LANES), F32)] + block_scratch,
        name="back",
    )(got_slots, dense_vectors, vectors, pairs, labels.reshape(1, samples), right, left, out_row)
    came = exchange(back.reshape(devices, capacity, width))
    came = came.reshape(devices * capacity, width)

    gathered = len(near_dense) * near_dense[0].shape[0]
    local = pl.pallas_call(
        functools.partial(top_kernel, len(near_dense)),
        out_shape=shape((inter + 8, hidden), F32),
        in_specs=[VMEM] * (2 * len(near_dense) + 2),
        out_specs=VMEM,
        scratch_shapes=[pltpu.VMEM((gathered, LANES), F32)] * 2,
        name="top",
    )(*near_dense, *near_pairs, right, out_row)
    summed = sum_rest(local)

    chunks = 4
    update = pl.pallas_call(
        functools.partial(update_kernel, capacity, chunks),
        out_shape=(shape((table_rows, width), F32), shape((table_rows // LANES, LANES), F32)),
        in_specs=[SMEM] + [VMEM] * 4,
        out_specs=(VMEM, VMEM),
        scratch_shapes=[pltpu.VMEM((bags, width), F32)],
        compiler_params=pltpu.CompilerParams(vmem_limit_bytes=24 << 20),
        name="update",
    )
    new_table, new_state = update(places, in_vmem(came), in_vmem(counts), in_vmem(held_table), held_state)
    return new_table, new_state.reshape(-1), summed[:inter], summed[inter]


def solution(mesh):
    both = P(AXES)
    in_specs = (P(AXES, None), both, P("gx"), both, P(AXES, None), P(AXES, None), both, P(AXES, None), both, P(), P())
    out_specs = (P(AXES, None), both, P(), P())
    return jax.shard_map(on_device, mesh=mesh, in_specs=in_specs, out_specs=out_specs, check_vma=False)
```

```python
import functools

import jax
import jax.numpy as jnp
from jax import lax
from jax.experimental import pallas as pl
from jax.experimental.pallas import tpu as pltpu
from jax.sharding import PartitionSpec as P


AXES = ("gx", "gy")
LANES = 128
TILE = 256
WINDOW = TILE + 8
learn_rate = 0.05
epsilon = 1e-08
HIGHEST = lax.Precision.HIGHEST
F32 = jnp.float32
BF16 = jnp.bfloat16
VMEM = pl.BlockSpec(memory_space=pltpu.VMEM)
SMEM = pl.BlockSpec(memory_space=pltpu.SMEM)
HBM = pl.BlockSpec(memory_space=pltpu.HBM)


def iota(shape, axis):
    return lax.broadcasted_iota(jnp.int32, shape, axis)


def ones_where(mask):
    return jnp.where(mask, 1.0, 0.0).astype(BF16)


def dot(a, b, **kw):
    return jnp.dot(a, b, preferred_element_type=F32, **kw)


def dot_t(a, b, **kw):
    return lax.dot_general(a, b, (((1,), (1,)), ((), ())), preferred_element_type=F32, **kw)


def split(x):
    high = x.astype(BF16)
    low = (x - high.astype(F32)).astype(BF16)
    return jnp.concatenate([high, low], axis=1)


def fold(x):
    half = x.shape[1] // 2
    return x[:, :half] + x[:, half:]


def prep_kernel(devices, capacity, features, look_ref, sizes_ref, owner_ref, slot_ref, dense_ref, labels_ref, meta_ref, slots_ref, bags_ref, told_ref):
    look_tiles = look_ref.shape[0]
    rows = sizes_ref.shape[0]
    samples = rows * LANES // features
    sizes = sizes_ref[...].astype(F32)
    owner = owner_ref[...]
    slot = slot_ref[...]
    lane_row, lane_col = iota((LANES, LANES), 0), iota((LANES, LANES), 1)
    upto = ones_where(lane_row <= lane_col)
    before = ones_where(lane_row < lane_col)
    every = jnp.ones((LANES, LANES), BF16)
    earlier = jnp.where(iota((rows, rows), 1) < iota((rows, rows), 0), 1.0, 0.0)
    sizes_b = sizes.astype(BF16)
    ends = dot(sizes_b, upto) + dot(earlier, dot(sizes_b, every), precision=HIGHEST)
    ends_i = ends.astype(jnp.int32)
    meta_ref[:look_tiles] = look_ref[...]
    meta_ref[look_tiles : look_tiles + rows] = (ends - sizes).astype(jnp.int32)
    meta_ref[look_tiles + rows : look_tiles + 2 * rows] = ends_i
    masks = [jnp.where(owner == d, 1.0, 0.0) for d in range(devices)]
    stack = jnp.concatenate(masks, axis=0).astype(BF16)
    ahead = dot(stack, before)
    total = dot(stack, every).astype(BF16)
    block = LANES // rows
    chain = ones_where((lane_row // rows == lane_col // rows) & (lane_col < lane_row))
    rank = jnp.zeros((rows, LANES), F32)
    for first in range(0, devices, block):
        part = slice(first * rows, (first + block) * rows)
        place = ahead[part] + dot(chain, total[part])
        for d in range(block):
            rank += masks[first + d] * place[d * rows : (d + 1) * rows]
    rank_i = rank.astype(jnp.int32)
    meta_ref[look_tiles + 2 * rows : look_tiles + 3 * rows] = owner * capacity + rank_i
    lane = iota((1, LANES), 1)
    starting = jnp.zeros((1, LANES), jnp.int32)
    for t in range(look_tiles * LANES // TILE):
        done = jnp.where(ends_i <= t * TILE, 1, 0)
        done = jnp.sum(jnp.sum(done, axis=0, keepdims=True), axis=1, keepdims=True)
        starting = jnp.where(lane == t, (done // 8) * 8, starting)
    meta_ref[look_tiles + 3 * rows :] = jnp.broadcast_to(starting, (8, LANES))
    where_to = (slot % features) * samples + slot // features
    high, low = (where_to // 64).astype(F32), (where_to % 64).astype(F32)
    found = jnp.zeros((5 * devices, LANES), F32)
    device_row = iota((devices, LANES), 0)
    across = iota((1, LANES), 1).astype(F32)
    for i in range(rows):
        mine = jnp.where(owner[i : i + 1] == device_row, 1.0, 0.0)
        left = jnp.concatenate(
            [mine * high[i : i + 1], mine * low[i : i + 1], mine, mine * float(i), mine * across], axis=0
        ).astype(BF16)
        found += dot_t(left, ones_where(rank_i[i : i + 1] == lane_row))
    found = [found[n * devices : (n + 1) * devices] for n in range(5)]
    slots_ref[...] = jnp.where(found[2] > 0.5, found[0] * 64 + found[1], -1.0).astype(jnp.int32)
    bags_ref[...] = jnp.where(found[2] > 0.5, found[3] * LANES + found[4], -1.0).astype(jnp.int32)
    told_ref[:samples] = dense_ref[...]
    told_ref[samples:] = jnp.broadcast_to(labels_ref[...], (8, LANES))


def column(row):
    return jnp.broadcast_to(row, (LANES, LANES)).T


def pool_kernel(look_tiles, rows, meta_s, meta_v, table, out, even, odd, pooled, first_k, last_k):
    bags = rows * LANES
    steps = look_tiles * LANES // TILE
    meta = meta_v[look_tiles : look_tiles + 2 * rows].astype(F32)
    for i in range(rows):
        at = slice(i * LANES, (i + 1) * LANES)
        first_k[at] = column(meta[i : i + 1])
        last_k[at] = column(meta[rows + i : rows + i + 1])
    first_k[bags:] = jnp.full((WINDOW, LANES), 1e9, F32)
    last_k[bags:] = jnp.full((WINDOW, LANES), -1.0, F32)
    pooled[...] = jnp.zeros_like(pooled)
    lane = iota((WINDOW, LANES), 1)

    def add_tile(t, source):
        window = pl.ds(pl.multiple_of(meta_s[look_tiles + 3 * rows, t], 8), WINDOW)
        first, last = first_k[window], last_k[window]
        parts = []
        for h in range(TILE // LANES):
            k = (lane + (t * TILE + h * LANES)).astype(F32)
            parts.append(ones_where((k >= first) & (k < last)))
        chosen = jnp.concatenate(parts, axis=1)
        pooled[window] += fold(dot(chosen, split(source[...])))

    def pick_tile(t, target):
        for c in range(TILE):
            target[c : c + 1] = table[pl.ds(meta_s[t * (TILE // LANES) + c // LANES, c % LANES], 1)]

    buffers = (even, odd)
    pick_tile(0, even)
    for t in range(1, steps):
        pick_tile(t, buffers[t % 2])
        add_tile(t - 1, buffers[(t - 1) % 2])
    add_tile(steps - 1, buffers[(steps - 1) % 2])

    for r in range(rows):
        for c in range(LANES):
            out[pl.ds(meta_s[look_tiles + 2 * rows + r, c], 1)] = pooled[r * LANES + c : r * LANES + c + 1]


def count_kernel(look_tiles, rows, meta_s, meta_v, out, total):
    i = pl.program_id(0)
    per = TILE // LANES
    start_row = look_tiles + i * per
    lowest = meta_s[start_row, 0]
    highest = meta_s[start_row + rows + per - 1, LANES - 1]
    starts = jnp.concatenate([meta_v[pl.ds(start_row + h, 1)] for h in range(per)], axis=1)
    ends = jnp.concatenate([meta_v[pl.ds(start_row + rows + h, 1)] for h in range(per)], axis=1)
    total[...] = jnp.zeros_like(total)

    @pl.loop(lowest // TILE, (highest + TILE - 1) // TILE)
    def _(c):
        look = jnp.concatenate([meta_v[pl.ds(c * per + h, 1)] for h in range(per)], axis=1)
        k = iota((TILE, TILE), 0) + c * TILE
        member = ones_where((k >= starts) & (k < ends))
        picked = ones_where(iota((total.shape[0], TILE), 0) == look)
        total[...] += dot(picked, member)

    out[...] = total[...].astype(BF16)


def pairs_of(features):
    return [(i, j) for i in range(features + 1) for j in range(i + 1, features + 1)]


def scatter_rows(places, source, capacity, blocks, target):
    for s in range(places.shape[0]):

        @pl.when(places[s, 0] >= 0)
        def _():
            part = blocks.at[pl.ds(pl.multiple_of(source(s) * capacity, 8), capacity)]
            for j in range(capacity):
                target[pl.ds(places[s, j], 1)] = part[j : j + 1]


def gram_kernel(features, capacity, slots, source, got, dense, turned, pairs, vectors, partial):
    samples = dense.shape[0]
    width = dense.shape[1]
    scatter_rows(slots, lambda s: source[s], capacity, got, vectors)
    turned[:width] = dense[...].T
    for f in range(features):
        turned[(f + 1) * width : (f + 2) * width] = vectors[f * samples : (f + 1) * samples].T
    p = 0
    for i in range(features):
        others = range(i + 1, features + 1)
        sums = {}
        for e in range(0, width, 8):
            mine = turned[i * width + e : i * width + e + 8]
            for j in others:
                term = mine * turned[j * width + e : j * width + e + 8]
                sums[j] = term if e == 0 else sums[j] + term
        for j in others:
            partial[p * 8 : p * 8 + 8] = sums[j]
            p += 1
    for q in range(0, p, 8):
        total = partial[pl.ds(q * 8, 8, 8)]
        for r in range(1, 8):
            total = total + partial[pl.ds(q * 8 + r, 8, 8)]
        pairs[q : q + 8] = total


def halves_of(x):
    high = x.astype(BF16)
    return high, (x - high.astype(F32)).astype(BF16)


def weight_kernel(weight, right, left):
    inter = weight.shape[0]
    dense_h, dense_l = halves_of(weight[:LANES])
    pairs_h, pairs_l = halves_of(weight[LANES : 2 * LANES])
    rest_h, rest_l = halves_of(weight[2 * LANES :])
    rest_h, rest_l = rest_h.astype(F32), rest_l.astype(F32)
    hidden = weight.shape[1]
    gap = jnp.zeros((LANES - 3 * (inter - 2 * LANES), hidden), F32)
    rest = jnp.concatenate([rest_h, rest_l, rest_h, gap], axis=0).astype(BF16)
    right[...] = jnp.concatenate([dense_h, pairs_h, dense_l, pairs_l, dense_h, pairs_h, rest], axis=0)
    gap = jnp.zeros((3 * LANES - inter, hidden), F32)
    tail_h = jnp.concatenate([rest_h, gap], axis=0).astype(BF16)
    tail_l = jnp.concatenate([rest_l, gap], axis=0).astype(BF16)
    for n, (head, tail) in enumerate(((pairs_h, tail_h), (pairs_l, tail_l), (pairs_h, tail_h))):
        left[:, n * hidden : (n + 1) * hidden] = jnp.concatenate([head, tail], axis=0)


def inputs_of(dense, told):
    samples = dense.shape[0]
    dense_h, dense_l = halves_of(dense)
    pairs_h, pairs_l = halves_of(told[:LANES].T)
    tail = told[LANES:]
    tail_h = tail.astype(BF16).astype(F32)
    gap = jnp.zeros((LANES - 3 * tail.shape[0], samples), F32)
    rest = jnp.concatenate([tail_h, tail_h, tail - tail_h, gap], axis=0).T.astype(BF16)
    return jnp.concatenate([dense_h, pairs_h, dense_h, pairs_h, dense_l, pairs_l, rest], axis=1)


def forward(x, labels, weight, out_weight):
    pre = dot(x, weight)
    gate = 1.0 / (1.0 + jnp.exp(-pre))
    hidden = pre * gate
    logits = jnp.sum(hidden * out_weight, axis=1, keepdims=True)
    d_logits = 1.0 / (1.0 + jnp.exp(-logits)) - labels
    d_pre = d_logits * out_weight * (gate + hidden * (1.0 - gate))
    return hidden, d_logits, d_pre


def back_kernel(features, capacity, slots, dense, turned, pairs, labels, weight, left, out_weight, back, d_vectors, d_turned, d_pairs, ready, sent):
    devices = slots.shape[0]
    samples, width = dense.shape
    x = inputs_of(dense[...], pairs[...])
    _, _, d_pre = forward(x, column(labels[...])[:, :1], weight[...], out_weight[...])
    high, low = halves_of(d_pre)
    d_pairs[...] = dot_t(left[: d_pairs.shape[0]], jnp.concatenate([high, high, low], axis=1))
    index = {pair: p for p, pair in enumerate(pairs_of(features))}

    @pl.loop(0, width // 8)
    def _(t):
        at = pl.multiple_of(t * 8, 8)
        each = [turned[pl.ds(f * width + at, 8)] for f in range(features + 1)]
        for f in range(1, features + 1):
            total = None
            for j in range(features + 1):
                if j != f:
                    slope = d_pairs[pl.ds(index[min(f, j), max(f, j)], 8, 0)]
                    term = slope * each[j]
                    total = term if total is None else total + term
            d_turned[pl.ds((f - 1) * width + at, 8)] = total

    for f in range(features):
        d_vectors[f * samples : (f + 1) * samples] = d_turned[f * width : (f + 1) * width].T

    def copy(s):
        part = pl.ds(pl.multiple_of(s * capacity, 8), capacity)
        return pltpu.make_async_copy(ready.at[part], back.at[part], sent.at[s])

    for s in range(devices):

        @pl.when(slots[s, 0] >= 0)
        def _(s=s):
            for j in range(s * capacity, (s + 1) * capacity):
                ready[j : j + 1] = d_vectors[pl.ds(slots[s, j - s * capacity], 1)]
            copy(s).start()

    @pl.loop(0, devices)
    def _(s):
        @pl.when(slots[s, 0] >= 0)
        def _():
            copy(s).wait()


def pack_kernel(*refs):
    size = refs[0].shape[0]
    for n, ref in enumerate(refs[:-1]):
        refs[-1][n * size : (n + 1) * size] = ref[...]


def top_kernel(dense_told, pairs_told, weight, out_weight, before, grad):
    inter = grad.shape[0] - 8
    block = LANES + inter - 2 * LANES
    xs, labels, columns = [], [], []
    for at in range(0, dense_told.shape[0], block):
        dense, told = dense_told[at : at + LANES], pairs_told[at : at + block]
        xs.append(inputs_of(dense, told))
        labels.append(column(dense_told[at + LANES : at + LANES + 1])[:, :1])
        columns.append(jnp.concatenate([dense.T, told, jnp.zeros((8, LANES), F32)], axis=0))
    hidden, d_logits, d_pre = forward(
        jnp.concatenate(xs, axis=0), jnp.concatenate(labels, axis=0), weight[...], out_weight[...]
    )
    x_high, x_low = halves_of(jnp.concatenate(columns, axis=1))
    d_high, d_low = halves_of(d_pre)
    total = dot(jnp.concatenate([x_high, x_high, x_low], axis=1), jnp.concatenate([d_high, d_low, d_high], axis=0))
    grad[:inter] = before[:inter] + total[:inter]
    last = jnp.sum(hidden * d_logits, axis=0, keepdims=True)
    grad[inter:] = before[inter:] + jnp.broadcast_to(last, (8, grad.shape[1]))


def update_kernel(capacity, bags_s, came, counts, table, state, new_table, new_state, grads, parts):
    @pl.when(pl.program_id(0) == 0)
    def _():
        scatter_rows(bags_s, lambda s: s, capacity, came, grads)
        parts[...] = split(grads[...])

    row_grad = fold(dot(counts[...], parts[...]))
    width = grads.shape[1]
    first = pl.program_id(0) * (counts.shape[0] // LANES)
    for j in range(counts.shape[0] // LANES):
        at = slice(j * LANES, (j + 1) * LANES)
        grad = row_grad[at]
        moved = column(state[pl.ds(first + j, 1)]) + jnp.sum(grad * grad, axis=1, keepdims=True) / width
        new_table[at] = table[at] - learn_rate * grad / (jnp.sqrt(moved) + epsilon)
        new_state[pl.ds(first + j, 1)] = moved.T[:1]


def trade(values, pair_value):
    result = values
    for bit in range(lax.axis_size("gy").bit_length() - 1):
        route = [(y, y ^ 1 << bit) for y in range(lax.axis_size("gy"))]
        partner = jax.tree.map(lambda x: lax.ppermute(x, "gy", route), result)
        flipped = jnp.bitwise_and(jnp.right_shift(pair_value, bit), 1) == 1
        result = jax.tree.map(functools.partial(jnp.where, flipped), partner, result)
    return result


def exchange(x):
    return lax.all_to_all(x, AXES, split_axis=0, concat_axis=0, tiled=True)


def in_vmem(value):
    return pltpu.with_memory_space_constraint(value, pltpu.VMEM)


def swap(value, offset):
    devices = lax.axis_size("gx") * lax.axis_size("gy")
    return lax.ppermute(value, AXES, [(d, d ^ offset) for d in range(devices)])


def gather_near(value):
    bits = (lax.axis_size("gx") * lax.axis_size("gy")).bit_length() - 1
    far = [value] + [swap(value, k << bits - 2) for k in range(1, 4)]
    value = pl.pallas_call(
        pack_kernel,
        out_shape=jax.ShapeDtypeStruct((4 * value.shape[0], value.shape[1]), value.dtype),
        in_specs=[VMEM] * 4,
        out_specs=VMEM,
        compiler_params=pltpu.CompilerParams(vmem_limit_bytes=4 << 20),
    )(*far)
    return [value] + [swap(value, k << bits - 4) for k in range(1, 4)]


def sum_rest(values):
    bits = (lax.axis_size("gx") * lax.axis_size("gy")).bit_length() - 1
    for bit in range(bits - 4):
        values = jax.tree.map(lambda x: x + swap(x, 1 << bit), values)
    return values


def on_device(
    emb_table, row_state, pair_mask, look_rows, bag_sizes, bag_owner, bag_slot, dense_vectors, labels, top_weight, out_weight
):
    groups_y = lax.axis_size("gy")
    devices = lax.axis_size("gx") * groups_y
    table_rows, width = emb_table.shape
    bags = bag_slot.shape[0]
    capacity = 2 * bags // devices
    samples = dense_vectors.shape[0]
    features = bags // samples
    look_tiles, rows = look_rows.shape[0] // LANES, bags // LANES
    inter, hidden = top_weight.shape
    pair_value = pair_mask[0]
    shape = jax.ShapeDtypeStruct

    tail = inter - 2 * LANES
    meta, slots, places, dense_told = pl.pallas_call(
        functools.partial(prep_kernel, devices, capacity, features),
        out_shape=(
            shape((look_tiles + 3 * rows + 8, LANES), jnp.int32),
            shape((devices, LANES), jnp.int32),
            shape((devices, LANES), jnp.int32),
            shape((samples + tail, width), F32),
        ),
        in_specs=[VMEM] * 6,
        out_specs=(VMEM,) * 4,
        name="prep",
    )(
        look_rows.reshape(look_tiles, LANES),
        bag_sizes.reshape(rows, LANES),
        bag_owner.reshape(rows, LANES),
        bag_slot.reshape(rows, LANES),
        dense_vectors,
        labels.reshape(1, samples),
    )
    traded_meta = trade(meta, pair_value)
    told = jnp.stack([slots[:, :capacity], jnp.full((devices, capacity), pair_value)], axis=1)
    told = exchange(told)
    got_slots = told[:, 0]
    source = jnp.bitwise_xor(jnp.arange(devices, dtype=jnp.int32), told[:, 1, 0])

    sent = pl.pallas_call(
        functools.partial(pool_kernel, look_tiles, rows),
        out_shape=shape((devices * capacity, width), F32),
        in_specs=[SMEM, VMEM, VMEM],
        out_specs=VMEM,
        scratch_shapes=[
            pltpu.VMEM((TILE, width), F32),
            pltpu.VMEM((TILE, width), F32),
            pltpu.VMEM((bags + WINDOW, width), F32),
            pltpu.VMEM((bags + WINDOW, LANES), F32),
            pltpu.VMEM((bags + WINDOW, LANES), F32),
        ],
        name="pool",
    )(traded_meta, traded_meta, emb_table)
    dense_told, sent = lax.optimization_barrier((dense_told, sent))
    got = exchange(sent.reshape(devices, capacity, width))
    got = got.reshape(devices * capacity, width)

    held_table = trade(emb_table, pair_value)
    held_state = trade(row_state.reshape(-1, LANES), pair_value)
    counts = pl.pallas_call(
        functools.partial(count_kernel, look_tiles, rows),
        out_shape=shape((table_rows, bags), BF16),
        grid=(bags // TILE,),
        in_specs=[SMEM, VMEM],
        out_specs=pl.BlockSpec((table_rows, TILE), lambda i: (0, i)),
        scratch_shapes=[pltpu.VMEM((table_rows, TILE), F32)],
        compiler_params=pltpu.CompilerParams(vmem_limit_bytes=24 << 20),
        name="count",
    )(meta, meta)

    right, left = pl.pallas_call(
        weight_kernel,
        out_shape=(shape((7 * LANES, hidden), BF16), shape((2 * LANES, 3 * hidden), BF16)),
        in_specs=[VMEM],
        out_specs=(VMEM, VMEM),
        compiler_params=pltpu.CompilerParams(vmem_limit_bytes=24 << 20),
        name="weights",
    )(top_weight)
    out_row = out_weight.reshape(1, hidden)
    pair_count = inter - width
    turned, pairs = pl.pallas_call(
        functools.partial(gram_kernel, features, capacity),
        out_shape=(shape((bags + samples, width), F32), shape((pair_count, samples), F32)),
        in_specs=[SMEM, SMEM, VMEM, VMEM],
        out_specs=(VMEM, VMEM),
        scratch_shapes=[pltpu.VMEM((bags, width), F32), pltpu.VMEM((8 * pair_count, samples), F32)],
        compiler_params=pltpu.CompilerParams(vmem_limit_bytes=16 << 20),
        name="gram",
    )(got_slots, source, in_vmem(got), dense_vectors)
    near_dense = gather_near(dense_told)
    near_pairs = gather_near(pairs)

    back = pl.pallas_call(
        functools.partial(back_kernel, features, capacity),
        out_shape=shape((devices * capacity, width), F32),
        in_specs=[SMEM] + [VMEM] * 7,
        out_specs=HBM,
        scratch_shapes=[
            pltpu.VMEM((bags, width), F32),
            pltpu.VMEM((bags, samples), F32),
            pltpu.VMEM((pair_count + 8, samples), F32),
            pltpu.VMEM((devices * capacity, width), F32),
            pltpu.SemaphoreType.DMA((devices,)),
        ],
        compiler_params=pltpu.CompilerParams(vmem_limit_bytes=58 << 20),
        name="back",
    )(
        got_slots,
        dense_vectors,
        in_vmem(turned),
        in_vmem(pairs),
        labels.reshape(1, samples),
        in_vmem(right),
        in_vmem(left),
        out_row,
    )
    came = exchange(back.reshape(devices, capacity, width))
    came = came.reshape(devices * capacity, width)

    local = jnp.zeros((inter + 8, hidden), F32)
    for dense_part, pairs_part in zip(near_dense, near_pairs):
        local = pl.pallas_call(
            top_kernel,
            out_shape=shape((inter + 8, hidden), F32),
            in_specs=[VMEM] * 5,
            out_specs=VMEM,
            compiler_params=pltpu.CompilerParams(vmem_limit_bytes=24 << 20),
            name="top",
        )(dense_part, pairs_part, right, out_row, local)
    top_grad, out_grad = sum_rest((local[:inter], local[inter]))

    chunks = 4
    piece = pl.BlockSpec((table_rows // chunks, width), lambda i: (i, 0))
    update = pl.pallas_call(
        functools.partial(update_kernel, capacity),
        out_shape=(shape((table_rows, width), F32), shape((table_rows // LANES, LANES), F32)),
        grid=(chunks,),
        in_specs=[SMEM, VMEM, pl.BlockSpec((table_rows // chunks, bags), lambda i: (i, 0)), piece, VMEM],
        out_specs=(piece, pl.BlockSpec((table_rows // LANES, LANES), lambda i: (0, 0))),
        scratch_shapes=[pltpu.VMEM((bags, width), F32), pltpu.VMEM((bags, 2 * width), BF16)],
        compiler_params=pltpu.CompilerParams(vmem_limit_bytes=56 << 20),
        name="update",
    )
    new_table, new_state = update(places, in_vmem(came), counts, held_table, held_state)
    return new_table, new_state.reshape(-1), top_grad, out_grad


def solution(mesh):
    both = P(AXES)
    in_specs = (P(AXES, None), both, P("gx"), both, P(AXES, None), P(AXES, None), both, P(AXES, None), both, P(), P())
    out_specs = (P(AXES, None), both, P(), P())
    return jax.shard_map(on_device, mesh=mesh, in_specs=in_specs, out_specs=out_specs, check_vma=False)
```

```python
import functools

import jax
import jax.numpy as jnp
from jax import lax
from jax.experimental import pallas as pl
from jax.experimental.pallas import tpu as pltpu
from jax.sharding import PartitionSpec as P


AXES = ("gx", "gy")
LANES = 128
TILE = 256
WINDOW = TILE + 8
learn_rate = 0.05
epsilon = 1e-08
HIGHEST = lax.Precision.HIGHEST
F32 = jnp.float32
BF16 = jnp.bfloat16
VMEM = pl.BlockSpec(memory_space=pltpu.VMEM)
SMEM = pl.BlockSpec(memory_space=pltpu.SMEM)
HBM = pl.BlockSpec(memory_space=pltpu.HBM)


def iota(shape, axis):
    return lax.broadcasted_iota(jnp.int32, shape, axis)


def ones_where(mask):
    return jnp.where(mask, 1.0, 0.0).astype(BF16)


def dot(a, b, **kw):
    return jnp.dot(a, b, preferred_element_type=F32, **kw)


def dot_t(a, b, **kw):
    return lax.dot_general(a, b, (((1,), (1,)), ((), ())), preferred_element_type=F32, **kw)


def split(x):
    high = x.astype(BF16)
    low = (x - high.astype(F32)).astype(BF16)
    return jnp.concatenate([high, low], axis=1)


def fold(x):
    half = x.shape[1] // 2
    return x[:, :half] + x[:, half:]


def prep_kernel(devices, capacity, features, look_ref, sizes_ref, owner_ref, slot_ref, dense_ref, labels_ref, meta_ref, slots_ref, bags_ref, told_ref):
    look_tiles = look_ref.shape[0]
    rows = sizes_ref.shape[0]
    samples = rows * LANES // features
    sizes = sizes_ref[...].astype(F32)
    owner = owner_ref[...]
    slot = slot_ref[...]
    lane_row, lane_col = iota((LANES, LANES), 0), iota((LANES, LANES), 1)
    upto = ones_where(lane_row <= lane_col)
    before = ones_where(lane_row < lane_col)
    every = jnp.ones((LANES, LANES), BF16)
    earlier = jnp.where(iota((rows, rows), 1) < iota((rows, rows), 0), 1.0, 0.0)
    sizes_b = sizes.astype(BF16)
    ends = dot(sizes_b, upto) + dot(earlier, dot(sizes_b, every), precision=HIGHEST)
    ends_i = ends.astype(jnp.int32)
    meta_ref[:look_tiles] = look_ref[...]
    meta_ref[look_tiles : look_tiles + rows] = (ends - sizes).astype(jnp.int32)
    meta_ref[look_tiles + rows : look_tiles + 2 * rows] = ends_i
    masks = [jnp.where(owner == d, 1.0, 0.0) for d in range(devices)]
    stack = jnp.concatenate(masks, axis=0).astype(BF16)
    ahead = dot(stack, before)
    total = dot(stack, every).astype(BF16)
    block = LANES // rows
    chain = ones_where((lane_row // rows == lane_col // rows) & (lane_col < lane_row))
    rank = jnp.zeros((rows, LANES), F32)
    for first in range(0, devices, block):
        part = slice(first * rows, (first + block) * rows)
        place = ahead[part] + dot(chain, total[part])
        for d in range(block):
            rank += masks[first + d] * place[d * rows : (d + 1) * rows]
    rank_i = rank.astype(jnp.int32)
    meta_ref[look_tiles + 2 * rows : look_tiles + 3 * rows] = owner * capacity + rank_i
    lane = iota((1, LANES), 1)
    starting = jnp.zeros((1, LANES), jnp.int32)
    for t in range(look_tiles * LANES // TILE):
        done = jnp.where(ends_i <= t * TILE, 1, 0)
        done = jnp.sum(jnp.sum(done, axis=0, keepdims=True), axis=1, keepdims=True)
        starting = jnp.where(lane == t, (done // 8) * 8, starting)
    meta_ref[look_tiles + 3 * rows :] = jnp.broadcast_to(starting, (8, LANES))
    where_to = (slot % features) * samples + slot // features
    high, low = (where_to // 64).astype(F32), (where_to % 64).astype(F32)
    found = jnp.zeros((5 * devices, LANES), F32)
    device_row = iota((devices, LANES), 0)
    across = iota((1, LANES), 1).astype(F32)
    for i in range(rows):
        mine = jnp.where(owner[i : i + 1] == device_row, 1.0, 0.0)
        left = jnp.concatenate(
            [mine * high[i : i + 1], mine * low[i : i + 1], mine, mine * float(i), mine * across], axis=0
        ).astype(BF16)
        found += dot_t(left, ones_where(rank_i[i : i + 1] == lane_row))
    found = [found[n * devices : (n + 1) * devices] for n in range(5)]
    slots_ref[...] = jnp.where(found[2] > 0.5, found[0] * 64 + found[1], -1.0).astype(jnp.int32)
    bags_ref[...] = jnp.where(found[2] > 0.5, found[3] * LANES + found[4], -1.0).astype(jnp.int32)
    told_ref[:samples] = dense_ref[...]
    told_ref[samples:] = jnp.broadcast_to(labels_ref[...], (8, LANES))


def column(row):
    return jnp.broadcast_to(row, (LANES, LANES)).T


def pool_kernel(look_tiles, rows, meta_s, meta_v, table, out, even, odd, pooled, first_k, last_k):
    bags = rows * LANES
    steps = look_tiles * LANES // TILE
    meta = meta_v[look_tiles : look_tiles + 2 * rows].astype(F32)
    for i in range(rows):
        at = slice(i * LANES, (i + 1) * LANES)
        first_k[at] = column(meta[i : i + 1])
        last_k[at] = column(meta[rows + i : rows + i + 1])
    first_k[bags:] = jnp.full((WINDOW, LANES), 1e9, F32)
    last_k[bags:] = jnp.full((WINDOW, LANES), -1.0, F32)
    pooled[...] = jnp.zeros_like(pooled)
    lane = iota((WINDOW, LANES), 1)

    def add_tile(t, source):
        window = pl.ds(pl.multiple_of(meta_s[look_tiles + 3 * rows, t], 8), WINDOW)
        first, last = first_k[window], last_k[window]
        parts = []
        for h in range(TILE // LANES):
            k = (lane + (t * TILE + h * LANES)).astype(F32)
            parts.append(ones_where((k >= first) & (k < last)))
        chosen = jnp.concatenate(parts, axis=1)
        pooled[window] += fold(dot(chosen, split(source[...])))

    def pick_tile(t, target):
        for c in range(TILE):
            target[c : c + 1] = table[pl.ds(meta_s[t * (TILE // LANES) + c // LANES, c % LANES], 1)]

    buffers = (even, odd)
    pick_tile(0, even)
    for t in range(1, steps):
        pick_tile(t, buffers[t % 2])
        add_tile(t - 1, buffers[(t - 1) % 2])
    add_tile(steps - 1, buffers[(steps - 1) % 2])

    for r in range(rows):
        for c in range(LANES):
            out[pl.ds(meta_s[look_tiles + 2 * rows + r, c], 1)] = pooled[r * LANES + c : r * LANES + c + 1]


def count_kernel(look_tiles, rows, meta_s, meta_v, out, total):
    i = pl.program_id(0)
    per = TILE // LANES
    start_row = look_tiles + i * per
    lowest = meta_s[start_row, 0]
    highest = meta_s[start_row + rows + per - 1, LANES - 1]
    starts = jnp.concatenate([meta_v[pl.ds(start_row + h, 1)] for h in range(per)], axis=1)
    ends = jnp.concatenate([meta_v[pl.ds(start_row + rows + h, 1)] for h in range(per)], axis=1)
    total[...] = jnp.zeros_like(total)

    @pl.loop(lowest // TILE, (highest + TILE - 1) // TILE)
    def _(c):
        look = jnp.concatenate([meta_v[pl.ds(c * per + h, 1)] for h in range(per)], axis=1)
        k = iota((TILE, TILE), 0) + c * TILE
        member = ones_where((k >= starts) & (k < ends))
        picked = ones_where(iota((total.shape[0], TILE), 0) == look)
        total[...] += dot(picked, member)

    out[...] = total[...].astype(BF16)


def pairs_of(features):
    return [(i, j) for i in range(features + 1) for j in range(i + 1, features + 1)]


def scatter_rows(places, source, capacity, blocks, target):
    for s in range(places.shape[0]):

        @pl.when(places[s, 0] >= 0)
        def _():
            part = blocks.at[pl.ds(pl.multiple_of(source(s) * capacity, 8), capacity)]
            for j in range(capacity):
                target[pl.ds(places[s, j], 1)] = part[j : j + 1]


def gram_kernel(features, capacity, slots, source, got, dense, turned, pairs, vectors, partial):
    samples = dense.shape[0]
    width = dense.shape[1]
    scatter_rows(slots, lambda s: source[s], capacity, got, vectors)
    turned[:width] = dense[...].T
    for f in range(features):
        turned[(f + 1) * width : (f + 2) * width] = vectors[f * samples : (f + 1) * samples].T
    p = 0
    for i in range(features):
        others = range(i + 1, features + 1)
        sums = {}
        for e in range(0, width, 8):
            mine = turned[i * width + e : i * width + e + 8]
            for j in others:
                term = mine * turned[j * width + e : j * width + e + 8]
                sums[j] = term if e == 0 else sums[j] + term
        for j in others:
            partial[p * 8 : p * 8 + 8] = sums[j]
            p += 1
    for q in range(0, p, 8):
        total = partial[pl.ds(q * 8, 8, 8)]
        for r in range(1, 8):
            total = total + partial[pl.ds(q * 8 + r, 8, 8)]
        pairs[q : q + 8] = total


def halves_of(x):
    high = x.astype(BF16)
    return high, (x - high.astype(F32)).astype(BF16)


def weight_kernel(weight, right, left):
    inter = weight.shape[0]
    dense_h, dense_l = halves_of(weight[:LANES])
    pairs_h, pairs_l = halves_of(weight[LANES : 2 * LANES])
    rest_h, rest_l = halves_of(weight[2 * LANES :])
    rest_h, rest_l = rest_h.astype(F32), rest_l.astype(F32)
    hidden = weight.shape[1]
    gap = jnp.zeros((LANES - 3 * (inter - 2 * LANES), hidden), F32)
    rest = jnp.concatenate([rest_h, rest_l, rest_h, gap], axis=0).astype(BF16)
    right[...] = jnp.concatenate([dense_h, pairs_h, dense_l, pairs_l, dense_h, pairs_h, rest], axis=0)
    gap = jnp.zeros((3 * LANES - inter, hidden), F32)
    tail_h = jnp.concatenate([rest_h, gap], axis=0).astype(BF16)
    tail_l = jnp.concatenate([rest_l, gap], axis=0).astype(BF16)
    for n, (head, tail) in enumerate(((pairs_h, tail_h), (pairs_l, tail_l), (pairs_h, tail_h))):
        left[:, n * hidden : (n + 1) * hidden] = jnp.concatenate([head, tail], axis=0)


def inputs_of(dense, told):
    samples = dense.shape[0]
    dense_h, dense_l = halves_of(dense)
    pairs_h, pairs_l = halves_of(told[:LANES].T)
    tail = told[LANES:]
    tail_h = tail.astype(BF16).astype(F32)
    gap = jnp.zeros((LANES - 3 * tail.shape[0], samples), F32)
    rest = jnp.concatenate([tail_h, tail_h, tail - tail_h, gap], axis=0).T.astype(BF16)
    return jnp.concatenate([dense_h, pairs_h, dense_h, pairs_h, dense_l, pairs_l, rest], axis=1)


def forward(x, labels, weight, out_weight):
    pre = dot(x, weight)
    gate = 1.0 / (1.0 + jnp.exp(-pre))
    hidden = pre * gate
    logits = jnp.sum(hidden * out_weight, axis=1, keepdims=True)
    d_logits = 1.0 / (1.0 + jnp.exp(-logits)) - labels
    d_pre = d_logits * out_weight * (gate + hidden * (1.0 - gate))
    return hidden, d_logits, d_pre


def back_kernel(features, capacity, slots, dense, turned, pairs, labels, weight, left, out_weight, back, d_vectors, d_turned, d_pairs, ready, sent):
    devices = slots.shape[0]
    samples, width = dense.shape
    x = inputs_of(dense[...], pairs[...])
    _, _, d_pre = forward(x, column(labels[...])[:, :1], weight[...], out_weight[...])
    high, low = halves_of(d_pre)
    d_pairs[...] = dot_t(left[: d_pairs.shape[0]], jnp.concatenate([high, high, low], axis=1))
    index = {pair: p for p, pair in enumerate(pairs_of(features))}

    @pl.loop(0, width // 8)
    def _(t):
        at = pl.multiple_of(t * 8, 8)
        each = [turned[pl.ds(f * width + at, 8)] for f in range(features + 1)]
        for f in range(1, features + 1):
            total = None
            for j in range(features + 1):
                if j != f:
                    slope = d_pairs[pl.ds(index[min(f, j), max(f, j)], 8, 0)]
                    term = slope * each[j]
                    total = term if total is None else total + term
            d_turned[pl.ds((f - 1) * width + at, 8)] = total

    for f in range(features):
        d_vectors[f * samples : (f + 1) * samples] = d_turned[f * width : (f + 1) * width].T

    def copy(s):
        part = pl.ds(pl.multiple_of(s * capacity, 8), capacity)
        return pltpu.make_async_copy(ready.at[part], back.at[part], sent.at[s])

    for s in range(devices):

        @pl.when(slots[s, 0] >= 0)
        def _(s=s):
            for j in range(s * capacity, (s + 1) * capacity):
                ready[j : j + 1] = d_vectors[pl.ds(slots[s, j - s * capacity], 1)]
            copy(s).start()

    @pl.loop(0, devices)
    def _(s):
        @pl.when(slots[s, 0] >= 0)
        def _():
            copy(s).wait()


def pack_kernel(*refs):
    size = refs[0].shape[0]
    for n, ref in enumerate(refs[:-1]):
        refs[-1][n * size : (n + 1) * size] = ref[...]


def top_kernel(dense_told, pairs_told, weight, out_weight, before, grad):
    inter = grad.shape[0] - 8
    block = LANES + inter - 2 * LANES
    xs, labels, columns = [], [], []
    for at in range(0, dense_told.shape[0], block):
        dense, told = dense_told[at : at + LANES], pairs_told[at : at + block]
        xs.append(inputs_of(dense, told))
        labels.append(column(dense_told[at + LANES : at + LANES + 1])[:, :1])
        columns.append(jnp.concatenate([dense.T, told, jnp.zeros((8, LANES), F32)], axis=0))
    hidden, d_logits, d_pre = forward(
        jnp.concatenate(xs, axis=0), jnp.concatenate(labels, axis=0), weight[...], out_weight[...]
    )
    x_high, x_low = halves_of(jnp.concatenate(columns, axis=1))
    d_high, d_low = halves_of(d_pre)
    total = dot(jnp.concatenate([x_high, x_high, x_low], axis=1), jnp.concatenate([d_high, d_low, d_high], axis=0))
    grad[:inter] = before[:inter] + total[:inter]
    last = jnp.sum(hidden * d_logits, axis=0, keepdims=True)
    grad[inter:] = before[inter:] + jnp.broadcast_to(last, (8, grad.shape[1]))


def update_kernel(capacity, bags_s, came, counts, table, state, new_table, new_state, grads, parts):
    @pl.when(pl.program_id(0) == 0)
    def _():
        scatter_rows(bags_s, lambda s: s, capacity, came, grads)
        parts[...] = split(grads[...])

    row_grad = fold(dot(counts[...], parts[...]))
    width = grads.shape[1]
    first = pl.program_id(0) * (counts.shape[0] // LANES)
    for j in range(counts.shape[0] // LANES):
        at = slice(j * LANES, (j + 1) * LANES)
        grad = row_grad[at]
        moved = column(state[pl.ds(first + j, 1)]) + jnp.sum(grad * grad, axis=1, keepdims=True) / width
        new_table[at] = table[at] - learn_rate * grad / (jnp.sqrt(moved) + epsilon)
        new_state[pl.ds(first + j, 1)] = moved.T[:1]


def trade(values, pair_value):
    result = values
    for bit in range(lax.axis_size("gy").bit_length() - 1):
        route = [(y, y ^ 1 << bit) for y in range(lax.axis_size("gy"))]
        partner = jax.tree.map(lambda x: lax.ppermute(x, "gy", route), result)
        flipped = jnp.bitwise_and(jnp.right_shift(pair_value, bit), 1) == 1
        result = jax.tree.map(functools.partial(jnp.where, flipped), partner, result)
    return result


def exchange(x):
    return lax.all_to_all(x, AXES, split_axis=0, concat_axis=0, tiled=True)


def in_vmem(value):
    return pltpu.with_memory_space_constraint(value, pltpu.VMEM)


def swap(value, offset):
    devices = lax.axis_size("gx") * lax.axis_size("gy")
    return lax.ppermute(value, AXES, [(d, d ^ offset) for d in range(devices)])


def gather_near(value):
    bits = (lax.axis_size("gx") * lax.axis_size("gy")).bit_length() - 1
    far = [value] + [swap(value, k << bits - 2) for k in range(1, 4)]
    value = pl.pallas_call(
        pack_kernel,
        out_shape=jax.ShapeDtypeStruct((4 * value.shape[0], value.shape[1]), value.dtype),
        in_specs=[VMEM] * 4,
        out_specs=VMEM,
        compiler_params=pltpu.CompilerParams(vmem_limit_bytes=4 << 20),
    )(*far)
    return [value] + [swap(value, k << bits - 4) for k in range(1, 4)]


def sum_rest(values):
    bits = (lax.axis_size("gx") * lax.axis_size("gy")).bit_length() - 1
    for bit in range(bits - 4):
        values = jax.tree.map(lambda x: x + swap(x, 1 << bit), values)
    return values


def on_device(
    emb_table, row_state, pair_mask, look_rows, bag_sizes, bag_owner, bag_slot, dense_vectors, labels, top_weight, out_weight
):
    groups_y = lax.axis_size("gy")
    devices = lax.axis_size("gx") * groups_y
    table_rows, width = emb_table.shape
    bags = bag_slot.shape[0]
    capacity = 2 * bags // devices
    samples = dense_vectors.shape[0]
    features = bags // samples
    look_tiles, rows = look_rows.shape[0] // LANES, bags // LANES
    inter, hidden = top_weight.shape
    pair_value = pair_mask[0]
    shape = jax.ShapeDtypeStruct

    tail = inter - 2 * LANES
    meta, slots, places, dense_told = pl.pallas_call(
        functools.partial(prep_kernel, devices, capacity, features),
        out_shape=(
            shape((look_tiles + 3 * rows + 8, LANES), jnp.int32),
            shape((devices, LANES), jnp.int32),
            shape((devices, LANES), jnp.int32),
            shape((samples + tail, width), F32),
        ),
        in_specs=[VMEM] * 6,
        out_specs=(VMEM,) * 4,
        name="prep",
    )(
        look_rows.reshape(look_tiles, LANES),
        bag_sizes.reshape(rows, LANES),
        bag_owner.reshape(rows, LANES),
        bag_slot.reshape(rows, LANES),
        dense_vectors,
        labels.reshape(1, samples),
    )
    traded_meta = trade(meta, pair_value)
    told = jnp.stack([slots[:, :capacity], jnp.full((devices, capacity), pair_value)], axis=1)
    told = exchange(told)
    got_slots = told[:, 0]
    source = jnp.bitwise_xor(jnp.arange(devices, dtype=jnp.int32), told[:, 1, 0])

    sent = pl.pallas_call(
        functools.partial(pool_kernel, look_tiles, rows),
        out_shape=shape((devices * capacity, width), F32),
        in_specs=[SMEM, VMEM, VMEM],
        out_specs=VMEM,
        scratch_shapes=[
            pltpu.VMEM((TILE, width), F32),
            pltpu.VMEM((TILE, width), F32),
            pltpu.VMEM((bags + WINDOW, width), F32),
            pltpu.VMEM((bags + WINDOW, LANES), F32),
            pltpu.VMEM((bags + WINDOW, LANES), F32),
        ],
        name="pool",
    )(traded_meta, traded_meta, emb_table)
    dense_told, sent = lax.optimization_barrier((dense_told, sent))
    got = exchange(sent.reshape(devices, capacity, width))
    got = got.reshape(devices * capacity, width)

    held_table = trade(emb_table, pair_value)
    held_state = trade(row_state.reshape(-1, LANES), pair_value)
    counts = pl.pallas_call(
        functools.partial(count_kernel, look_tiles, rows),
        out_shape=shape((table_rows, bags), BF16),
        grid=(bags // TILE,),
        in_specs=[SMEM, VMEM],
        out_specs=pl.BlockSpec((table_rows, TILE), lambda i: (0, i)),
        scratch_shapes=[pltpu.VMEM((table_rows, TILE), F32)],
        compiler_params=pltpu.CompilerParams(vmem_limit_bytes=24 << 20),
        name="count",
    )(meta, meta)

    right, left = pl.pallas_call(
        weight_kernel,
        out_shape=(shape((7 * LANES, hidden), BF16), shape((2 * LANES, 3 * hidden), BF16)),
        in_specs=[VMEM],
        out_specs=(VMEM, VMEM),
        compiler_params=pltpu.CompilerParams(vmem_limit_bytes=24 << 20),
        name="weights",
    )(top_weight)
    out_row = out_weight.reshape(1, hidden)
    pair_count = inter - width
    turned, pairs = pl.pallas_call(
        functools.partial(gram_kernel, features, capacity),
        out_shape=(shape((bags + samples, width), F32), shape((pair_count, samples), F32)),
        in_specs=[SMEM, SMEM, VMEM, VMEM],
        out_specs=(VMEM, VMEM),
        scratch_shapes=[pltpu.VMEM((bags, width), F32), pltpu.VMEM((8 * pair_count, samples), F32)],
        compiler_params=pltpu.CompilerParams(vmem_limit_bytes=16 << 20),
        name="gram",
    )(got_slots, source, in_vmem(got), dense_vectors)
    near_dense = gather_near(dense_told)
    near_pairs = gather_near(pairs)

    back = pl.pallas_call(
        functools.partial(back_kernel, features, capacity),
        out_shape=shape((devices * capacity, width), F32),
        in_specs=[SMEM] + [VMEM] * 7,
        out_specs=HBM,
        scratch_shapes=[
            pltpu.VMEM((bags, width), F32),
            pltpu.VMEM((bags, samples), F32),
            pltpu.VMEM((pair_count + 8, samples), F32),
            pltpu.VMEM((devices * capacity, width), F32),
            pltpu.SemaphoreType.DMA((devices,)),
        ],
        compiler_params=pltpu.CompilerParams(vmem_limit_bytes=58 << 20),
        name="back",
    )(
        got_slots,
        dense_vectors,
        in_vmem(turned),
        in_vmem(pairs),
        labels.reshape(1, samples),
        in_vmem(right),
        in_vmem(left),
        out_row,
    )
    came = exchange(back.reshape(devices, capacity, width))
    came = came.reshape(devices * capacity, width)

    local = jnp.zeros((inter + 8, hidden), F32)
    for dense_part, pairs_part in zip(near_dense, near_pairs):
        local = pl.pallas_call(
            top_kernel,
            out_shape=shape((inter + 8, hidden), F32),
            in_specs=[VMEM] * 5,
            out_specs=VMEM,
            compiler_params=pltpu.CompilerParams(vmem_limit_bytes=24 << 20),
            name="top",
        )(dense_part, pairs_part, right, out_row, local)
    top_grad, out_grad = sum_rest((local[:inter], local[inter]))

    chunks = 4
    piece = pl.BlockSpec((table_rows // chunks, width), lambda i: (i, 0))
    update = pl.pallas_call(
        functools.partial(update_kernel, capacity),
        out_shape=(shape((table_rows, width), F32), shape((table_rows // LANES, LANES), F32)),
        grid=(chunks,),
        in_specs=[SMEM, VMEM, pl.BlockSpec((table_rows // chunks, bags), lambda i: (i, 0)), piece, VMEM],
        out_specs=(piece, pl.BlockSpec((table_rows // LANES, LANES), lambda i: (0, 0))),
        scratch_shapes=[pltpu.VMEM((bags, width), F32), pltpu.VMEM((bags, 2 * width), BF16)],
        compiler_params=pltpu.CompilerParams(vmem_limit_bytes=24 << 20),
        name="update",
    )
    new_table, new_state = update(
        places, in_vmem(came), pltpu.with_memory_space_constraint(counts, pltpu.HBM), held_table, held_state
    )
    return new_table, new_state.reshape(-1), top_grad, out_grad


def solution(mesh):
    both = P(AXES)
    in_specs = (P(AXES, None), both, P("gx"), both, P(AXES, None), P(AXES, None), both, P(AXES, None), both, P(), P())
    out_specs = (P(AXES, None), both, P(), P())
    return jax.shard_map(on_device, mesh=mesh, in_specs=in_specs, out_specs=out_specs, check_vma=False)
```
